768 devices in a mesh: slab: 12 (over z), inner: 64 (over x, y, core).
Axes of the slice: x: 4, y: 8, z: 12, core: 2. Of those that a mesh axis runs over, the one named last changes fastest.
Arguments:
- matrix_blocks: bfloat16 [12288, 27, 64, 64], P(('slab', 'inner')), may hold values from -6 to 6
- prolong: bfloat16 [12288, 64, 64], P(('slab', 'inner')), may hold values from -0.75 to 0.75
- columns: int32 [12288, 27], P(('slab', 'inner')), may hold values from 0 to 12287, as said below
- partial_slot: int32 [12288, 27], P(('slab', 'inner')), may hold values from 0 to 47
- into_slot: int32 [768, 48], P(('slab', 'inner')), may hold values from 0 to 31
Outputs:
- coarse: float32 [24576, 4096], P(('slab', 'inner'))
The draws below stay inside these ranges and needn't reach their ends.
Inputs may be any that keep to these rules, and one draw needn't show every extreme that they name: `columns`: A slab's block rows form a periodic grid of 2 x 64 x (8) blocks: row s * 1024 + q * 16 + x * 8 + z sits at (x, q, z). Entry [i, 0] is i itself; entries 1 to 26 are the 26 grid neighbours of i (offsets -1, 0, 1 in each dimension, modulo the grid), in an order drawn for each row.
All inputs are finite; a program needn't handle non-finite values.
Results may differ from the reference program's by a relative error of at most 0.0029.
Values may be sent and summed in bfloat16 or wider, within the bound.
No kernel may reach another device: no remote copies, remote signals or barrier semaphores. Data moves between devices by JAX's collectives and lax.ppermute only.
A program may use at most 128 MiB of HBM per device.

```python
import math
import jax
import jax.numpy as jnp
import numpy as np
from jax import lax

BW = 64
NBR = 27
ROWS_DEV = 16
BUF = 16
SLOTS = 32
FINE = 12288
N_SLAB = 12
N_INNER = 64
DEVICES = 768


def draw_columns(key, part):
    half = ROWS_DEV // 2
    group_size = ROWS_DEV * N_INNER
    offsets = [(0, 0, 0)]
    for step_x in (-1, 0, 1):
        for step_y in (-1, 0, 1):
            for step_z in (-1, 0, 1):
                if (step_x, step_y, step_z) != (0, 0, 0):
                    offsets.append((step_x, step_y, step_z))
    offset_table = np.array(offsets, dtype=np.int32)
    row_ids = jnp.arange(FINE, dtype=jnp.int32)
    slab_base = row_ids // group_size * group_size
    within = row_ids % group_size
    layer_y = within // ROWS_DEV
    local_row = within % ROWS_DEV
    layer_x = local_row // half
    layer_z = local_row % half
    new_x = (layer_x[:, None] + jnp.asarray(offset_table[:, 0])[None, :]) % 2
    new_y = (layer_y[:, None] + jnp.asarray(offset_table[:, 1])[None, :]) % N_INNER
    new_z = (layer_z[:, None] + jnp.asarray(offset_table[:, 2])[None, :]) % half
    neighbours = slab_base[:, None] + new_y * ROWS_DEV + new_x * half + new_z
    scores = jax.random.randint(key, (FINE, NBR - 1), 0, 1 << 20, dtype=jnp.int32) * 32 + jnp.arange(NBR - 1, dtype=jnp.int32)[None, :]
    order = jnp.argsort(scores, axis=1).astype(jnp.int32)
    shuffled = jnp.take_along_axis(neighbours[:, 1:], order, axis=1)
    return jnp.concatenate([neighbours[:, :1], shuffled], axis=1).astype(jnp.int32)


def set_ends(values, own_key, least, high):
    longest = values.shape.index(max(values.shape))
    spots = []
    for shift in (0, 1):
        where = [jax.random.randint(jax.random.fold_in(own_key, axis), (), 0, length) for axis, length in enumerate(values.shape)]
        where[longest] = (where[longest] + shift) % values.shape[longest]
        spots.append(tuple(where))
    return values.at[spots[0]].set(least).at[spots[1]].set(high)


def steps_of(key, shape, split, smallest, high):
    def one(position, shards_of):
        draws = jax.random.uniform(jax.random.fold_in(jax.random.fold_in(key, 6), position), (shards_of,), jnp.float32, smallest / len(split), high / len(split))
        return jnp.repeat(jnp.exp(draws), shape[position] // shards_of).reshape((-1,) + (1,) * (len(shape) - position - 1))

    factor_of = one(*split[0])
    for cut in split[1:]:
        factor_of = factor_of * one(*cut)
    return factor_of


def rank_bounds(count, skew):
    portions = [(1 << 20) // math.isqrt(standing ** skew) + 1 for standing in range(1, count + 1)]
    deviation = 1 + sum(portions) // (1 << 30)
    return np.cumsum(np.array([max(1, weight // deviation) for weight in portions]))


def ranked(own_key, shape, amount, skew):
    listing = rank_bounds(amount, skew)
    lot = jax.random.randint(jax.random.fold_in(own_key, 1), shape, 0, int(listing[amount - 1]))
    standing = jnp.searchsorted(jnp.asarray(listing, jnp.int32), lot, side="right")
    return jax.random.permutation(jax.random.fold_in(own_key, 2), amount)[standing].astype(jnp.int32)


def noise(rng, shape, spread, limit, pieces=(), held_as=jnp.bfloat16):
    values = jax.random.normal(rng, shape, jnp.float32) * spread
    if len(pieces) > 0:
        values = steps_of(rng, shape, pieces, -0.22, 0.18) * values
    return jnp.clip(values, min=-limit, max=limit).astype(held_as)


def setup_inputs(seed: int = 0) -> dict:
    arg_keys = jax.random.split(jax.random.key(seed), 6)
    return {
        "matrix_blocks": noise(arg_keys[0], (FINE, NBR, BW, BW), 1.0, 6.0, ((0, 768),)),
        "prolong": noise(arg_keys[1], (FINE, BW, BW), 0.125, 0.75, ((0, 768),)),
        "columns": draw_columns(jax.random.fold_in(arg_keys[5], 71), 0),
        "partial_slot": set_ends(ranked(arg_keys[3], (FINE, NBR), 3 * BUF, 2), jax.random.fold_in(arg_keys[3], 3), 0, (3 * BUF) - 1).astype(jnp.int32),
        "into_slot": set_ends(jax.random.randint(arg_keys[4], (DEVICES, 3 * BUF), 0, SLOTS), jax.random.fold_in(arg_keys[4], 1), 0, SLOTS - 1).astype(jnp.int32),
    }


def partials_of(mat_blocks, own_blocks, picked, slot_ids):
    row_count = own_blocks.shape[0]
    left_mat = mat_blocks.astype(jnp.float32)
    right_mat = picked.reshape(row_count, NBR, BW, BW).astype(jnp.float32)
    applied = jnp.einsum("rkab,rkbc->rkac", left_mat, right_mat, precision=lax.Precision.HIGHEST).astype(jnp.bfloat16)
    contrib = jnp.einsum("rab,rkac->rkbc", own_blocks.astype(jnp.float32), applied.astype(jnp.float32), precision=lax.Precision.HIGHEST)
    chooser = (slot_ids[:, :, None] == jnp.arange(3 * BUF, dtype=jnp.int32)[None, None, :]).astype(jnp.float32)
    summed = jnp.einsum("rkm,rkbc->mbc", chooser, contrib, precision=lax.Precision.HIGHEST)
    return summed.reshape(3 * BUF, BW * BW)


def reference(matrix_blocks, prolong, columns, partial_slot, into_slot):
    device_count = N_SLAB * N_INNER

    def per_device(index):
        base = (index * ROWS_DEV).astype(jnp.int32)
        mat_blocks = lax.dynamic_slice_in_dim(matrix_blocks, base, ROWS_DEV, 0)
        own_blocks = lax.dynamic_slice_in_dim(prolong, base, ROWS_DEV, 0)
        col_ids = lax.dynamic_slice_in_dim(columns, base, ROWS_DEV, 0)
        slot_ids = lax.dynamic_slice_in_dim(partial_slot, base, ROWS_DEV, 0)
        picked = jnp.take(prolong, col_ids.reshape(-1), axis=0)
        return partials_of(mat_blocks, own_blocks, picked, slot_ids)

    partial_value = lax.map(per_device, jnp.arange(device_count, dtype=jnp.int32))
    slab_grid = partial_value.reshape(N_SLAB, N_INNER, 3 * BUF, BW * BW)
    from_left = jnp.roll(slab_grid[:, :, 2 * BUF:], 1, axis=0)
    from_right = jnp.roll(slab_grid[:, :, :BUF], -1, axis=0)
    incoming = jnp.concatenate([from_left, slab_grid[:, :, BUF:2 * BUF], from_right], axis=2)
    incoming = incoming.reshape(device_count, 3 * BUF, BW * BW)
    chooser = (into_slot[:, None, :] == jnp.arange(SLOTS, dtype=jnp.int32)[None, :, None]).astype(jnp.float32)
    coarse = jnp.einsum("dsm,dmx->dsx", chooser, incoming, precision=lax.Precision.HIGHEST)
    return coarse.reshape(device_count * SLOTS, BW * BW)
```

```python
import jax
import jax.numpy as jnp
from jax import lax
from jax.experimental import pallas as pl
from jax.experimental.pallas import tpu as pltpu
from jax.sharding import PartitionSpec as P

BUF = 16
SLOTS = 32


def shifted(value, axis, steps):
    count = lax.axis_size(axis)
    pairs = [(source, (source + steps) % count) for source in range(count)]
    return lax.ppermute(value, axis, pairs)


def triple_kernel(layer_ref, cols, slots, before, own, after, blocks, out, wide):
    rows, per_row = cols.shape
    layers = layer_ref[1]
    wide[:rows] = before[...]
    wide[rows : 2 * rows] = own[...]
    wide[2 * rows :] = after[...]
    out[...] = jnp.zeros_like(out)

    def row(i, carry):
        left = own[i].T
        for k in range(per_row):
            col = cols[i, k]
            layer = lax.rem(lax.div(col, rows) - layer_ref[0] + layers, layers)
            place = layer * rows + lax.rem(col, rows)
            applied = jnp.dot(blocks[i, k], wide[place], preferred_element_type=jnp.float32)
            contrib = jnp.dot(left, applied.astype(jnp.bfloat16), preferred_element_type=jnp.float32)
            slot = slots[i, k]
            out[slot] = out[slot] + contrib
        return carry

    lax.fori_loop(0, rows, row, 0)


def per_device(matrix_blocks, prolong, columns, partial_slot, into_slot):
    rows, width = prolong.shape[:2]
    layers = lax.axis_size("inner")
    before = shifted(prolong, "inner", 1)
    after = shifted(prolong, "inner", -1)
    first = lax.rem(lax.axis_index("inner") + layers - 1, layers)
    base = first + lax.axis_index("slab") * layers
    layer_info = jnp.stack([base, jnp.int32(layers)]).astype(jnp.int32)
    smem = pl.BlockSpec(memory_space=pltpu.SMEM)
    vmem = pl.BlockSpec(memory_space=pltpu.VMEM)
    partial_value = pl.pallas_call(
        triple_kernel,
        out_shape=jax.ShapeDtypeStruct((3 * BUF, width, width), jnp.float32),
        in_specs=[smem, smem, smem, vmem, vmem, vmem, vmem],
        out_specs=vmem,
        scratch_shapes=[pltpu.VMEM((3 * rows, width, width), jnp.bfloat16)],
        compiler_params=pltpu.CompilerParams(vmem_limit_bytes=24 << 20),
        name="triple",
    )(layer_info, columns, partial_slot, before, prolong, after, matrix_blocks)
    partial_value = partial_value.reshape(3 * BUF, width * width)
    from_left = shifted(partial_value[2 * BUF :].astype(jnp.bfloat16), "slab", 1)
    from_right = shifted(partial_value[:BUF].astype(jnp.bfloat16), "slab", -1)
    picks = into_slot[0][None, :] == jnp.arange(SLOTS, dtype=jnp.int32)[:, None]
    kept = jnp.dot(
        picks[:, BUF : 2 * BUF].astype(jnp.float32),
        partial_value[BUF : 2 * BUF],
        precision=lax.Precision.HIGHEST,
    )
    sides = jnp.concatenate([picks[:, :BUF], picks[:, 2 * BUF :]], axis=1).astype(jnp.bfloat16)
    arrived = jnp.concatenate([from_left, from_right], axis=0)
    return kept + jnp.dot(sides, arrived, preferred_element_type=jnp.float32)


def solution(mesh):
    return jax.shard_map(
        per_device,
        mesh=mesh,
        in_specs=(
            P(("slab", "inner"), None, None, None),
            P(("slab", "inner"), None, None),
            P(("slab", "inner"), None),
            P(("slab", "inner"), None),
            P(("slab", "inner"), None),
        ),
        out_specs=P(("slab", "inner"), None),
        check_vma=False,
    )
```

```python
import jax
import jax.numpy as jnp
from jax import lax
from jax.experimental import pallas as pl
from jax.experimental.pallas import tpu as pltpu
from jax.sharding import PartitionSpec as P

W = 64
HALF = W // 2
LANES = 2 * W
NBR = 27
ROWS = 16
DEPTH = 8
BUF = 16
SLOTS = 32
LAYERS = 64
F32 = jnp.float32
BF = jnp.bfloat16
UNROLL_NEAR, UNROLL_FAR, UNROLL_STRIP = 8, 4, 8


def shifted(value, axis, steps):
    count = lax.axis_size(axis)
    pairs = [(source, (source + steps) % count) for source in range(count)]
    return lax.ppermute(value, axis, pairs)


def ordered(cols, slots):
    row = lax.broadcasted_iota(jnp.int32, cols.shape, 0)
    k = lax.broadcasted_iota(jnp.int32, cols.shape, 1)
    layer = (cols >> 4) & (LAYERS - 1)
    own = jnp.broadcast_to(layer[:, 0:1], cols.shape)
    d = (layer - own + 1) & (LAYERS - 1)
    other = ((cols >> 3) & 1) ^ (row >> 3)
    g = ((cols & 7) - (row & 7) + 1) & 7
    key = d * 6 + other * 3 + g
    value = (k * W + slots).astype(F32)
    table = jnp.zeros(cols.shape, F32)
    for d in range(3):
        for g in range(3):
            one = jnp.min(jnp.where(key == d * 6 + g, value, 1e9), axis=1, keepdims=True)
            two = key == d * 6 + 3 + g
            low = jnp.min(jnp.where(two, value, 1e9), axis=1, keepdims=True)
            high = jnp.max(jnp.where(two, value, -1.0), axis=1, keepdims=True)
            for u, found in enumerate((one, low, high)):
                table = jnp.where(k == d * 9 + u * 3 + g, found, table)
    return table.astype(jnp.int32)


def user(x, u, g, z):
    return (x if u == 0 else 1 - x) * DEPTH + ((z - g + 1) & (DEPTH - 1))


def add_to(acc, slot, value):
    spot = acc.at[pl.ds(pl.multiple_of(slot * HALF, HALF), HALF), :]
    spot[...] = spot[...] + value


def add_strip(left, strip, accs, slot_of, count):
    both = jnp.dot(left, strip, preferred_element_type=F32)
    low = lax.broadcasted_iota(jnp.int32, (HALF, LANES), 1) < W
    for e in range(0, count, 2):
        even = both[:HALF, W * e : W * e + LANES]
        odd = both[HALF:, W * e : W * e + LANES]
        add_to(accs[0], slot_of(e), jnp.where(low, even, pltpu.roll(odd, W, 1)))
        if e + 1 < count:
            add_to(accs[1], slot_of(e + 1), jnp.where(low, pltpu.roll(even, W, 1), odd))


def near_kernel(
    blocks, own, cols, slots, far, acc_a, acc_b, table, left,
    held, prolong, cols_v, slots_v, look, double, strip, sems, row_sems,
):
    small = [
        pltpu.make_async_copy(source, target, sems.at[n])
        for n, (source, target) in enumerate(((cols, cols_v), (slots, slots_v), (own, prolong)))
    ]
    for copy in small:
        copy.start()

    def fetches(z):
        return [
            pltpu.make_async_copy(blocks.at[i], held.at[i], row_sems.at[i]) for i in (z, z + DEPTH)
        ]

    for z in (7, 0, 1, 2, 3, 4, 5, 6):
        for copy in fetches(z):
            copy.start()
    acc_a[...] = jnp.zeros_like(acc_a)
    acc_b[...] = jnp.zeros_like(acc_b)
    small[0].wait()
    small[1].wait()
    table[...] = ordered(cols_v[...], slots_v[...])
    to_look = pltpu.make_async_copy(table, look, sems.at[3])
    to_look.start()
    small[2].wait()
    r = lax.broadcasted_iota(jnp.int32, (W, W), 0)
    c = lax.broadcasted_iota(jnp.int32, (W, W), 1)
    split = (c == (r % HALF) * 2 + r // HALF).astype(F32).astype(BF)
    for i in range(ROWS):
        p = prolong[i]
        double[i] = jnp.concatenate([p, p], axis=1)
        left[i] = lax.dot_general(
            split, p, (((1,), (1,)), ((), ())), preferred_element_type=F32
        ).astype(BF)
    to_look.wait()

    def block(i, d, u, g):
        return held[i, look[i, d * 9 + u * 3 + g] >> 6]

    def repack(z):
        for copy in fetches(z):
            copy.wait()
        for x in range(2):
            for u in range(3):
                for g in range(3):
                    at = (u * 3 + g) * W
                    side = LANES * (x if u == 0 else 1 - x)
                    i = x * DEPTH + z
                    pair = jnp.concatenate([block(i, 0, u, g), block(i, 2, u, g)], axis=1)
                    far[(z + g - 1) & (DEPTH - 1), at : at + W, side : side + LANES] = pair

    repack(7)
    repack(0)
    for z in range(DEPTH):
        if z < DEPTH - 2:
            repack(z + 1)
        for x in range(2):
            users = [(user(x, u, g, z), u, g) for u in range(3) for g in range(3)]
            stack = jnp.concatenate([block(i, 1, u, g) for i, u, g in users], axis=0)
            applied = jnp.dot(stack, double[x * DEPTH + z], preferred_element_type=F32).astype(BF)
            for e, (i, u, g) in enumerate(users):
                lane = W * (e % 2)
                strip[i, :, W * e : W * e + W] = applied[W * e : W * e + W, lane : lane + W]

    def finish(i, carry):
        add_strip(left[i], strip[i], (acc_a, acc_b), lambda e: look[i, 9 + e] & (W - 1), 9)
        return carry

    lax.fori_loop(0, ROWS, finish, 0, unroll=UNROLL_NEAR)


def far_kernel(
    table, blocks, near_a, near_b, left, before, after, up, mid, down,
    acc_a, acc_b, look, lows, highs, strip, sems,
):
    to_look = pltpu.make_async_copy(table, look, sems.at[0])
    to_look.start()
    none = jnp.zeros((W, W), BF)
    blank = jnp.zeros((W, LANES), BF)
    for j in range(ROWS):
        lows[j] = jnp.concatenate([before[j], none], axis=1)
        highs[j] = jnp.concatenate([none, after[j]], axis=1)
    part = acc_a.shape[0] // DEPTH

    def multiply(z, carry):
        rows = pl.ds(pl.multiple_of(z * part, part), part)
        acc_a[rows, :] = near_a[rows, :]
        acc_b[rows, :] = near_b[rows, :]
        four = [
            jnp.concatenate([lows[z], blank], axis=1),
            jnp.concatenate([highs[z], blank], axis=1),
            jnp.concatenate([blank, lows[DEPTH + z]], axis=1),
            jnp.concatenate([blank, highs[DEPTH + z]], axis=1),
        ]
        diagonal = jnp.concatenate(four, axis=0)
        applied = jnp.dot(blocks[z], diagonal, preferred_element_type=F32).astype(BF)
        for u in range(3):
            for g in range(3):
                at = (u * 3 + g) * W
                for x in range(2):
                    part_of = applied[at : at + W, LANES * x : LANES * x + LANES]
                    strip[user(x, u, g, z), :, 2 * at : 2 * at + LANES] = part_of
        return carry

    lax.fori_loop(0, DEPTH, multiply, 0, unroll=UNROLL_FAR)
    to_look.wait()

    def finish(i, carry):
        add_strip(
            left[i], strip[i], (acc_a, acc_b), lambda e: look[i, e // 2 + 18 * (e % 2)] & (W - 1), 18
        )
        return carry

    lax.fori_loop(0, ROWS, finish, 0, unroll=UNROLL_STRIP)
    for n, out in enumerate((down, mid, up)):
        rows = slice(n * BUF * HALF, (n + 1) * BUF * HALF)
        out[...] = (acc_a[rows, :] + acc_b[rows, :]).astype(out.dtype)


def gather_kernel(into, left, mid, right, out, acc):
    acc[...] = jnp.zeros_like(acc)
    for n, source in enumerate((left, mid, right)):
        for m in range(BUF):
            add_to(acc, into[0, n * BUF + m], source[HALF * m : HALF * m + HALF, :].astype(F32))
    out[...] = acc[...].reshape(out.shape)


def per_device(matrix_blocks, prolong, columns, partial_slot, into_slot):
    before = shifted(prolong, "inner", 1)
    after = shifted(prolong, "inner", -1)
    hbm = pl.BlockSpec(memory_space=pltpu.HBM)
    vmem = pl.BlockSpec(memory_space=pltpu.VMEM)
    smem = pl.BlockSpec(memory_space=pltpu.SMEM)
    sums = jax.ShapeDtypeStruct((3 * BUF * HALF, LANES), F32)
    third = (BUF * HALF, LANES)
    sent = jax.ShapeDtypeStruct(third, BF)
    table_v = pltpu.VMEM((ROWS, NBR), jnp.int32)
    table_s = pltpu.SMEM((ROWS, NBR), jnp.int32)
    wide = pltpu.VMEM((ROWS, W, LANES), BF)
    far, acc_a, acc_b, table, left = pl.pallas_call(
        near_kernel,
        out_shape=(
            jax.ShapeDtypeStruct((DEPTH, 9 * W, 4 * W), BF),
            sums,
            sums,
            jax.ShapeDtypeStruct((ROWS, NBR), jnp.int32),
            jax.ShapeDtypeStruct((ROWS, W, W), BF),
        ),
        in_specs=[hbm] * 4,
        out_specs=(vmem,) * 5,
        scratch_shapes=[
            pltpu.VMEM((ROWS, NBR, W, W), BF),
            pltpu.VMEM((ROWS, W, W), BF),
            table_v,
            table_v,
            table_s,
            wide,
            pltpu.VMEM((ROWS, W, 10 * W), BF),
            pltpu.SemaphoreType.DMA((4,)),
            pltpu.SemaphoreType.DMA((ROWS,)),
        ],
        compiler_params=pltpu.CompilerParams(vmem_limit_bytes=46 << 20),
        cost_estimate=pl.CostEstimate(flops=10**9, bytes_accessed=12 * 10**6, transcendentals=0),
        name="near",
    )(matrix_blocks, prolong, columns, partial_slot)
    up, mid, down = pl.pallas_call(
        far_kernel,
        out_shape=(sent, jax.ShapeDtypeStruct(third, F32), sent),
        in_specs=[vmem] * 7,
        out_specs=(vmem,) * 3,
        scratch_shapes=[
            pltpu.VMEM(sums.shape, F32),
            pltpu.VMEM(sums.shape, F32),
            table_s,
            wide,
            wide,
            pltpu.VMEM((ROWS, W, 18 * W), BF),
            pltpu.SemaphoreType.DMA((1,)),
        ],
        compiler_params=pltpu.CompilerParams(vmem_limit_bytes=24 << 20),
        name="far",
    )(table, far, acc_a, acc_b, left, before, after)
    from_left = shifted(up, "slab", 1)
    from_right = shifted(down, "slab", -1)
    return pl.pallas_call(
        gather_kernel,
        out_shape=jax.ShapeDtypeStruct((SLOTS, W * W), F32),
        in_specs=[smem, vmem, vmem, vmem],
        out_specs=vmem,
        scratch_shapes=[pltpu.VMEM((SLOTS * HALF, LANES), F32)],
        compiler_params=pltpu.CompilerParams(vmem_limit_bytes=16 << 20),
        name="gather",
    )(into_slot, from_left, mid, from_right)


def solution(mesh):
    return jax.shard_map(
        per_device,
        mesh=mesh,
        in_specs=(
            P(("slab", "inner"), None, None, None),
            P(("slab", "inner"), None, None),
            P(("slab", "inner"), None),
            P(("slab", "inner"), None),
            P(("slab", "inner"), None),
        ),
        out_specs=P(("slab", "inner"), None),
        check_vma=False,
    )
```

```python
import jax
import jax.numpy as jnp
from jax import lax
from jax.experimental import pallas as pl
from jax.experimental.pallas import tpu as pltpu
from jax.sharding import PartitionSpec as P

W = 64
HALF = W // 2
LANES = 2 * W
NBR = 27
ROWS = 16
DEPTH = 8
BUF = 16
SLOTS = 32
LAYERS = 64
F32 = jnp.float32
BF = jnp.bfloat16
UNROLL_NEAR, UNROLL_FAR, UNROLL_STRIP = 8, 4, 8


def shifted(value, axis, steps):
    count = lax.axis_size(axis)
    pairs = [(source, (source + steps) % count) for source in range(count)]
    return lax.ppermute(value, axis, pairs)


def ordered(cols, slots):
    row = lax.broadcasted_iota(jnp.int32, cols.shape, 0)
    k = lax.broadcasted_iota(jnp.int32, cols.shape, 1)
    layer = (cols >> 4) & (LAYERS - 1)
    own = jnp.broadcast_to(layer[:, 0:1], cols.shape)
    d = (layer - own + 1) & (LAYERS - 1)
    other = ((cols >> 3) & 1) ^ (row >> 3)
    g = ((cols & 7) - (row & 7) + 1) & 7
    key = d * 6 + other * 3 + g
    value = (k * W + slots).astype(F32)
    table = jnp.zeros(cols.shape, F32)
    for d in range(3):
        for g in range(3):
            one = jnp.min(jnp.where(key == d * 6 + g, value, 1e9), axis=1, keepdims=True)
            two = key == d * 6 + 3 + g
            low = jnp.min(jnp.where(two, value, 1e9), axis=1, keepdims=True)
            high = jnp.max(jnp.where(two, value, -1.0), axis=1, keepdims=True)
            for u, found in enumerate((one, low, high)):
                table = jnp.where(k == d * 9 + u * 3 + g, found, table)
    return table.astype(jnp.int32)


def user(x, u, g, z):
    return (x if u == 0 else 1 - x) * DEPTH + ((z - g + 1) & (DEPTH - 1))


def add_to(acc, slot, value):
    spot = acc.at[pl.ds(pl.multiple_of(slot * HALF, HALF), HALF), :]
    spot[...] = spot[...] + value


def add_strip(left, strip, accs, slot_of, count):
    both = jnp.dot(left, strip, preferred_element_type=F32)
    low = lax.broadcasted_iota(jnp.int32, (HALF, LANES), 1) < W
    for e in range(0, count, 2):
        even = both[:HALF, W * e : W * e + LANES]
        odd = both[HALF:, W * e : W * e + LANES]
        add_to(accs[0], slot_of(e), jnp.where(low, even, pltpu.roll(odd, W, 1)))
        if e + 1 < count:
            add_to(accs[1], slot_of(e + 1), jnp.where(low, pltpu.roll(even, W, 1), odd))


def near_kernel(
    blocks, own, cols, slots, far, acc_a, acc_b, table, left,
    held, prolong, cols_v, slots_v, look, double, strip, sems, row_sems,
):
    small = [
        pltpu.make_async_copy(source, target, sems.at[n])
        for n, (source, target) in enumerate(((cols, cols_v), (slots, slots_v), (own, prolong)))
    ]
    for copy in small:
        copy.start()

    def fetches(z):
        return [
            pltpu.make_async_copy(blocks.at[i], held.at[i], row_sems.at[i]) for i in (z, z + DEPTH)
        ]

    for z in (7, 0, 1, 2, 3, 4, 5, 6):
        for copy in fetches(z):
            copy.start()
    acc_a[...] = jnp.zeros_like(acc_a)
    acc_b[...] = jnp.zeros_like(acc_b)
    small[0].wait()
    small[1].wait()
    table[...] = ordered(cols_v[...], slots_v[...])
    to_look = pltpu.make_async_copy(table, look, sems.at[3])
    to_look.start()
    small[2].wait()
    r = lax.broadcasted_iota(jnp.int32, (W, W), 0)
    c = lax.broadcasted_iota(jnp.int32, (W, W), 1)
    split = (c == (r % HALF) * 2 + r // HALF).astype(F32).astype(BF)
    for i in range(ROWS):
        p = prolong[i]
        double[i] = jnp.concatenate([p, p], axis=1)
        left[i] = lax.dot_general(
            split, p, (((1,), (1,)), ((), ())), preferred_element_type=F32
        ).astype(BF)
    to_look.wait()

    def block(i, d, u, g):
        return held[i, look[i, d * 9 + u * 3 + g] >> 6]

    def repack(z):
        for copy in fetches(z):
            copy.wait()
        for x in range(2):
            for u in range(3):
                for g in range(3):
                    at = (u * 3 + g) * W
                    side = LANES * (x if u == 0 else 1 - x)
                    i = x * DEPTH + z
                    pair = jnp.concatenate([block(i, 0, u, g), block(i, 2, u, g)], axis=1)
                    far[(z + g - 1) & (DEPTH - 1), at : at + W, side : side + LANES] = pair

    repack(7)
    repack(0)
    for z in range(DEPTH):
        if z < DEPTH - 2:
            repack(z + 1)
        for x in range(2):
            users = [(user(x, u, g, z), u, g) for u in range(3) for g in range(3)]
            stack = jnp.concatenate([block(i, 1, u, g) for i, u, g in users], axis=0)
            applied = jnp.dot(stack, double[x * DEPTH + z], preferred_element_type=F32).astype(BF)
            for e, (i, u, g) in enumerate(users):
                lane = W * (e % 2)
                strip[i, :, W * e : W * e + W] = applied[W * e : W * e + W, lane : lane + W]

    def finish(i, carry):
        add_strip(left[i], strip[i], (acc_a, acc_b), lambda e: look[i, 9 + e] & (W - 1), 9)
        return carry

    lax.fori_loop(0, ROWS, finish, 0, unroll=UNROLL_NEAR)


def far_kernel(
    table, blocks, near_a, near_b, left, before, after, up, mid, down,
    acc_a, acc_b, look, lows, highs, strip, sems,
):
    to_look = pltpu.make_async_copy(table, look, sems.at[0])
    to_look.start()
    none = jnp.zeros((W, W), BF)
    blank = jnp.zeros((W, LANES), BF)
    for j in range(ROWS):
        lows[j] = jnp.concatenate([before[j], none], axis=1)
        highs[j] = jnp.concatenate([none, after[j]], axis=1)
    part = acc_a.shape[0] // DEPTH

    def multiply(z, carry):
        rows = pl.ds(pl.multiple_of(z * part, part), part)
        acc_a[rows, :] = near_a[rows, :]
        acc_b[rows, :] = near_b[rows, :]
        four = [
            jnp.concatenate([lows[z], blank], axis=1),
            jnp.concatenate([highs[z], blank], axis=1),
            jnp.concatenate([blank, lows[DEPTH + z]], axis=1),
            jnp.concatenate([blank, highs[DEPTH + z]], axis=1),
        ]
        diagonal = jnp.concatenate(four, axis=0)
        applied = jnp.dot(blocks[z], diagonal, preferred_element_type=F32).astype(BF)
        for u in range(3):
            for g in range(3):
                at = (u * 3 + g) * W
                for x in range(2):
                    part_of = applied[at : at + W, LANES * x : LANES * x + LANES]
                    strip[user(x, u, g, z), :, 2 * at : 2 * at + LANES] = part_of
        return carry

    lax.fori_loop(0, DEPTH, multiply, 0, unroll=UNROLL_FAR)
    to_look.wait()

    def finish(i, carry):
        add_strip(
            left[i], strip[i], (acc_a, acc_b), lambda e: look[i, e // 2 + 18 * (e % 2)] & (W - 1), 18
        )
        return carry

    lax.fori_loop(0, ROWS, finish, 0, unroll=UNROLL_STRIP)
    for n, out in enumerate((down, mid, up)):
        rows = slice(n * BUF * HALF, (n + 1) * BUF * HALF)
        out[...] = (acc_a[rows, :] + acc_b[rows, :]).astype(out.dtype)


def gather_kernel(into, left, mid, right, out, acc):
    acc[...] = jnp.zeros_like(acc)
    for n, source in enumerate((left, mid, right)):
        for m in range(BUF):
            add_to(acc, into[0, n * BUF + m], source[HALF * m : HALF * m + HALF, :].astype(F32))
    out[...] = acc[...].reshape(out.shape)


def per_device(matrix_blocks, prolong, columns, partial_slot, into_slot):
    before = shifted(prolong, "inner", 1)
    after = shifted(prolong, "inner", -1)
    hbm = pl.BlockSpec(memory_space=pltpu.HBM)
    vmem = pl.BlockSpec(memory_space=pltpu.VMEM)
    smem = pl.BlockSpec(memory_space=pltpu.SMEM)
    sums = jax.ShapeDtypeStruct((3 * BUF * HALF, LANES), F32)
    third = (BUF * HALF, LANES)
    sent = jax.ShapeDtypeStruct(third, BF)
    table_v = pltpu.VMEM((ROWS, NBR), jnp.int32)
    table_s = pltpu.SMEM((ROWS, NBR), jnp.int32)
    wide = pltpu.VMEM((ROWS, W, LANES), BF)
    far, acc_a, acc_b, table, left = pl.pallas_call(
        near_kernel,
        out_shape=(
            jax.ShapeDtypeStruct((DEPTH, 9 * W, 4 * W), BF),
            sums,
            sums,
            jax.ShapeDtypeStruct((ROWS, NBR), jnp.int32),
            jax.ShapeDtypeStruct((ROWS, W, W), BF),
        ),
        in_specs=[hbm] * 4,
        out_specs=(vmem,) * 5,
        scratch_shapes=[
            pltpu.VMEM((ROWS, NBR, W, W), BF),
            pltpu.VMEM((ROWS, W, W), BF),
            table_v,
            table_v,
            table_s,
            wide,
            pltpu.VMEM((ROWS, W, 10 * W), BF),
            pltpu.SemaphoreType.DMA((4,)),
            pltpu.SemaphoreType.DMA((ROWS,)),
        ],
        compiler_params=pltpu.CompilerParams(vmem_limit_bytes=46 << 20),
        cost_estimate=pl.CostEstimate(flops=10**9, bytes_accessed=12 * 10**6, transcendentals=0),
        name="near",
    )(*(pltpu.with_memory_space_constraint(v, pltpu.HBM) for v in (matrix_blocks, prolong, columns, partial_slot)))
    up, mid, down = pl.pallas_call(
        far_kernel,
        out_shape=(sent, jax.ShapeDtypeStruct(third, F32), sent),
        in_specs=[vmem] * 7,
        out_specs=(vmem,) * 3,
        scratch_shapes=[
            pltpu.VMEM(sums.shape, F32),
            pltpu.VMEM(sums.shape, F32),
            table_s,
            wide,
            wide,
            pltpu.VMEM((ROWS, W, 18 * W), BF),
            pltpu.SemaphoreType.DMA((1,)),
        ],
        compiler_params=pltpu.CompilerParams(vmem_limit_bytes=24 << 20),
        name="far",
    )(table, far, acc_a, acc_b, left, before, after)
    from_left = shifted(up, "slab", 1)
    from_right = shifted(down, "slab", -1)
    return pl.pallas_call(
        gather_kernel,
        out_shape=jax.ShapeDtypeStruct((SLOTS, W * W), F32),
        in_specs=[smem, vmem, vmem, vmem],
        out_specs=vmem,
        scratch_shapes=[pltpu.VMEM((SLOTS * HALF, LANES), F32)],
        compiler_params=pltpu.CompilerParams(vmem_limit_bytes=16 << 20),
        name="gather",
    )(into_slot, from_left, mid, from_right)


def solution(mesh):
    return jax.shard_map(
        per_device,
        mesh=mesh,
        in_specs=(
            P(("slab", "inner"), None, None, None),
            P(("slab", "inner"), None, None),
            P(("slab", "inner"), None),
            P(("slab", "inner"), None),
            P(("slab", "inner"), None),
        ),
        out_specs=P(("slab", "inner"), None),
        check_vma=False,
    )
```

```python
import jax
import jax.numpy as jnp
from jax import lax
from jax.experimental import pallas as pl
from jax.experimental.pallas import tpu as pltpu
from jax.sharding import PartitionSpec as P

W = 64
HALF = W // 2
LANES = 2 * W
NBR = 27
ROWS = 16
DEPTH = 8
BUF = 16
SLOTS = 32
LAYERS = 64
F32 = jnp.float32
BF = jnp.bfloat16
UNROLL_FAR, UNROLL_STRIP = 8, 8
STEPS = (
    ((7, 0, 1), (0,), ()),
    ((2, 3), (1, 2), ()),
    ((4, 5), (3, 4), (1,)),
    ((6,), (5, 6, 7), (2, 3)),
    ((), (), (0, 4, 5, 6, 7)),
)


def shifted(value, axis, steps):
    count = lax.axis_size(axis)
    pairs = [(source, (source + steps) % count) for source in range(count)]
    return lax.ppermute(value, axis, pairs)


def ordered(cols, slots):
    row = lax.broadcasted_iota(jnp.int32, cols.shape, 0)
    k = lax.broadcasted_iota(jnp.int32, cols.shape, 1)
    layer = (cols >> 4) & (LAYERS - 1)
    own = jnp.broadcast_to(layer[:, 0:1], cols.shape)
    d = (layer - own + 1) & (LAYERS - 1)
    other = ((cols >> 3) & 1) ^ (row >> 3)
    g = ((cols & 7) - (row & 7) + 1) & 7
    key = d * 6 + other * 3 + g
    value = (k * W + slots).astype(F32)
    table = jnp.zeros(cols.shape, F32)
    for d in range(3):
        for g in range(3):
            one = jnp.min(jnp.where(key == d * 6 + g, value, 1e9), axis=1, keepdims=True)
            two = key == d * 6 + 3 + g
            low = jnp.min(jnp.where(two, value, 1e9), axis=1, keepdims=True)
            high = jnp.max(jnp.where(two, value, -1.0), axis=1, keepdims=True)
            for u, found in enumerate((one, low, high)):
                table = jnp.where(k == d * 9 + u * 3 + g, found, table)
    return table.astype(jnp.int32)


def user(x, u, g, z):
    return (x if u == 0 else 1 - x) * DEPTH + ((z - g + 1) & (DEPTH - 1))


def add_to(acc, slot, value):
    spot = acc.at[pl.ds(pl.multiple_of(slot * HALF, HALF), HALF), :]
    spot[...] = spot[...] + value


def add_strip(left, strip, accs, slot_of, count):
    both = jnp.dot(left, strip, preferred_element_type=F32)
    low = lax.broadcasted_iota(jnp.int32, (HALF, LANES), 1) < W
    for e in range(0, count, 2):
        even = both[:HALF, W * e : W * e + LANES]
        odd = both[HALF:, W * e : W * e + LANES]
        add_to(accs[0], slot_of(e), jnp.where(low, even, pltpu.roll(odd, W, 1)))
        if e + 1 < count:
            add_to(accs[1], slot_of(e + 1), jnp.where(low, pltpu.roll(even, W, 1), odd))


def near_kernel(
    blocks, own, cols, slots, far, acc_a, acc_b, table, left,
    held, prolong, cols_v, slots_v, look, double, strip, sems, row_sems,
):
    small = [
        pltpu.make_async_copy(source, target, sems.at[n])
        for n, (source, target) in enumerate(((cols, cols_v), (slots, slots_v), (own, prolong)))
    ]
    for copy in small:
        copy.start()

    def fetches(z):
        return [
            pltpu.make_async_copy(blocks.at[i], held.at[i], row_sems.at[i]) for i in (z, z + DEPTH)
        ]

    for z in (7, 0, 1, 2, 3, 4, 5, 6):
        for copy in fetches(z):
            copy.start()
    acc_a[...] = jnp.zeros_like(acc_a)
    acc_b[...] = jnp.zeros_like(acc_b)
    small[0].wait()
    small[1].wait()
    table[...] = ordered(cols_v[...], slots_v[...])
    to_look = pltpu.make_async_copy(table, look, sems.at[3])
    to_look.start()
    small[2].wait()
    r = lax.broadcasted_iota(jnp.int32, (W, W), 0)
    c = lax.broadcasted_iota(jnp.int32, (W, W), 1)
    split = (c == (r % HALF) * 2 + r // HALF).astype(F32).astype(BF)
    for i in range(ROWS):
        p = prolong[i]
        double[i] = jnp.concatenate([p, p], axis=1)
        left[i] = lax.dot_general(
            split, p, (((1,), (1,)), ((), ())), preferred_element_type=F32
        ).astype(BF)
    to_look.wait()

    def block(i, d, u, g):
        return held[i, look[i, d * 9 + u * 3 + g] >> 6]

    def repack(z):
        for x in range(2):
            for u in range(3):
                for g in range(3):
                    at = (u * 3 + g) * W
                    side = LANES * (x if u == 0 else 1 - x)
                    i = x * DEPTH + z
                    pair = jnp.concatenate([block(i, 0, u, g), block(i, 2, u, g)], axis=1)
                    far[(z + g - 1) & (DEPTH - 1), at : at + W, side : side + LANES] = pair

    def local(z):
        for x in range(2):
            users = [(user(x, u, g, z), u, g) for u in range(3) for g in range(3)]
            stack = jnp.concatenate([block(i, 1, u, g) for i, u, g in users], axis=0)
            applied = jnp.dot(stack, double[x * DEPTH + z], preferred_element_type=F32).astype(BF)
            for e, (i, u, g) in enumerate(users):
                lane = W * (e % 2)
                strip[i, :, W * e : W * e + W] = applied[W * e : W * e + W, lane : lane + W]

    def finish(z):
        for i in (z, z + DEPTH):
            add_strip(left[i], strip[i], (acc_a, acc_b), lambda e: look[i, 9 + e] & (W - 1), 9)

    for arrived, complete, ready in STEPS:
        for z in arrived:
            for copy in fetches(z):
                copy.wait()
        for z in ready:
            finish(z)
        for z in arrived:
            repack(z)
        for z in complete:
            local(z)


def far_kernel(
    table, blocks, near_a, near_b, left, after, before, up, mid, down,
    acc_a, acc_b, look, lows, highs, strip, sems,
):
    to_look = pltpu.make_async_copy(table, look, sems.at[0])
    to_look.start()
    none = jnp.zeros((W, W), BF)
    blank = jnp.zeros((W, LANES), BF)
    for j in range(ROWS):
        lows[j] = jnp.concatenate([before[j], none], axis=1)
        highs[j] = jnp.concatenate([none, after[j]], axis=1)
    part = acc_a.shape[0] // DEPTH

    def multiply(z, carry):
        rows = pl.ds(pl.multiple_of(z * part, part), part)
        acc_a[rows, :] = near_a[rows, :]
        acc_b[rows, :] = near_b[rows, :]
        four = [
            jnp.concatenate([lows[z], blank], axis=1),
            jnp.concatenate([highs[z], blank], axis=1),
            jnp.concatenate([blank, lows[DEPTH + z]], axis=1),
            jnp.concatenate([blank, highs[DEPTH + z]], axis=1),
        ]
        diagonal = jnp.concatenate(four, axis=0)
        applied = jnp.dot(blocks[z], diagonal, preferred_element_type=F32).astype(BF)
        for u in range(3):
            for g in range(3):
                at = (u * 3 + g) * W
                for x in range(2):
                    part_of = applied[at : at + W, LANES * x : LANES * x + LANES]
                    strip[user(x, u, g, z), :, 2 * at : 2 * at + LANES] = part_of
        return carry

    lax.fori_loop(0, DEPTH, multiply, 0, unroll=UNROLL_FAR)
    to_look.wait()

    def finish(i, carry):
        add_strip(
            left[i], strip[i], (acc_a, acc_b), lambda e: look[i, e // 2 + 18 * (e % 2)] & (W - 1), 18
        )
        return carry

    lax.fori_loop(0, ROWS, finish, 0, unroll=UNROLL_STRIP)
    for n, out in enumerate((down, mid, up)):
        rows = slice(n * BUF * HALF, (n + 1) * BUF * HALF)
        out[...] = (acc_a[rows, :] + acc_b[rows, :]).astype(out.dtype)


def gather_kernel(into, left, mid, right, out, acc):
    acc[...] = jnp.zeros_like(acc)
    for n, source in enumerate((left, mid, right)):
        for m in range(BUF):
            add_to(acc, into[0, n * BUF + m], source[HALF * m : HALF * m + HALF, :].astype(F32))
    out[...] = acc[...].reshape(out.shape)


HBM = pl.BlockSpec(memory_space=pltpu.HBM)
VMEM = pl.BlockSpec(memory_space=pltpu.VMEM)
SMEM = pl.BlockSpec(memory_space=pltpu.SMEM)
SUMS = jax.ShapeDtypeStruct((3 * BUF * HALF, LANES), F32)
THIRD = (BUF * HALF, LANES)
TABLE = (ROWS, NBR)
WIDE = pltpu.VMEM((ROWS, W, LANES), BF)


def near(*operands):
    return pl.pallas_call(
        near_kernel,
        out_shape=(
            jax.ShapeDtypeStruct((DEPTH, 9 * W, 4 * W), BF),
            SUMS,
            SUMS,
            jax.ShapeDtypeStruct(TABLE, jnp.int32),
            jax.ShapeDtypeStruct((ROWS, W, W), BF),
        ),
        in_specs=[HBM] * 4,
        out_specs=(VMEM,) * 5,
        scratch_shapes=[
            pltpu.VMEM((ROWS, NBR, W, W), BF),
            pltpu.VMEM((ROWS, W, W), BF),
            pltpu.VMEM(TABLE, jnp.int32),
            pltpu.VMEM(TABLE, jnp.int32),
            pltpu.SMEM(TABLE, jnp.int32),
            WIDE,
            pltpu.VMEM((ROWS, W, 10 * W), BF),
            pltpu.SemaphoreType.DMA((4,)),
            pltpu.SemaphoreType.DMA((ROWS,)),
        ],
        compiler_params=pltpu.CompilerParams(vmem_limit_bytes=40 << 20),
        cost_estimate=pl.CostEstimate(flops=10**9, bytes_accessed=12 * 10**6, transcendentals=0),
        name="near",
    )(*(pltpu.with_memory_space_constraint(value, pltpu.HBM) for value in operands))


def far(*operands):
    sent = jax.ShapeDtypeStruct(THIRD, BF)
    return pl.pallas_call(
        far_kernel,
        out_shape=(sent, jax.ShapeDtypeStruct(THIRD, F32), sent),
        in_specs=[VMEM] * 7,
        out_specs=(VMEM,) * 3,
        scratch_shapes=[
            pltpu.VMEM(SUMS.shape, F32),
            pltpu.VMEM(SUMS.shape, F32),
            pltpu.SMEM(TABLE, jnp.int32),
            WIDE,
            WIDE,
            pltpu.VMEM((ROWS, W, 18 * W), BF),
            pltpu.SemaphoreType.DMA((1,)),
        ],
        compiler_params=pltpu.CompilerParams(vmem_limit_bytes=24 << 20),
        name="far",
    )(*operands)


def gather(*operands):
    return pl.pallas_call(
        gather_kernel,
        out_shape=jax.ShapeDtypeStruct((SLOTS, W * W), F32),
        in_specs=[SMEM, VMEM, VMEM, VMEM],
        out_specs=VMEM,
        scratch_shapes=[pltpu.VMEM((SLOTS * HALF, LANES), F32)],
        compiler_params=pltpu.CompilerParams(vmem_limit_bytes=16 << 20),
        name="gather",
    )(*operands)


def per_device(matrix_blocks, prolong, columns, partial_slot, into_slot):
    before = shifted(prolong, "inner", 1)
    after = shifted(prolong, "inner", -1)
    blocks, acc_a, acc_b, table, left = near(matrix_blocks, prolong, columns, partial_slot)
    up, mid, down = far(table, blocks, acc_a, acc_b, left, after, before)
    from_left = shifted(up, "slab", 1)
    from_right = shifted(down, "slab", -1)
    return gather(into_slot, from_left, mid, from_right)


def solution(mesh):
    return jax.shard_map(
        per_device,
        mesh=mesh,
        in_specs=(
            P(("slab", "inner"), None, None, None),
            P(("slab", "inner"), None, None),
            P(("slab", "inner"), None),
            P(("slab", "inner"), None),
            P(("slab", "inner"), None),
        ),
        out_specs=P(("slab", "inner"), None),
        check_vma=False,
    )
```

```python
import jax
import jax.numpy as jnp
from jax import lax
from jax.experimental import pallas as pl
from jax.experimental.pallas import tpu as pltpu
from jax.sharding import PartitionSpec as P

W = 64
HALF = W // 2
LANES = 2 * W
NBR = 27
ROWS = 16
DEPTH = 8
BUF = 16
SLOTS = 32
LAYERS = 64
F32 = jnp.float32
BF = jnp.bfloat16
UNROLL_FAR, UNROLL_STRIP = 8, 16
AHEAD = 4
STEPS = (
    ((7, 0), (), ()),
    ((1,), (0,), ()),
    ((2,), (1,), ()),
    ((3,), (2,), ()),
    ((4,), (3,), (1,)),
    ((5,), (4,), (2,)),
    ((6,), (5, 6, 7), (3,)),
    ((), (), (0, 4, 5, 6, 7)),
)


def shifted(value, axis, steps):
    count = lax.axis_size(axis)
    pairs = [(source, (source + steps) % count) for source in range(count)]
    return lax.ppermute(value, axis, pairs)


def ordered(cols, slots):
    row = lax.broadcasted_iota(jnp.int32, cols.shape, 0)
    k = lax.broadcasted_iota(jnp.int32, cols.shape, 1)
    layer = (cols >> 4) & (LAYERS - 1)
    own = jnp.broadcast_to(layer[:, 0:1], cols.shape)
    d = (layer - own + 1) & (LAYERS - 1)
    other = ((cols >> 3) & 1) ^ (row >> 3)
    g = ((cols & 7) - (row & 7) + 1) & 7
    key = d * 6 + other * 3 + g
    value = (k * W + slots).astype(F32)
    table = jnp.zeros(cols.shape, F32)
    for d in range(3):
        for g in range(3):
            one = jnp.min(jnp.where(key == d * 6 + g, value, 1e9), axis=1, keepdims=True)
            two = key == d * 6 + 3 + g
            low = jnp.min(jnp.where(two, value, 1e9), axis=1, keepdims=True)
            high = jnp.max(jnp.where(two, value, -1.0), axis=1, keepdims=True)
            for u, found in enumerate((one, low, high)):
                table = jnp.where(k == d * 9 + u * 3 + g, found, table)
    return table.astype(jnp.int32)


def user(x, u, g, z):
    return (x if u == 0 else 1 - x) * DEPTH + ((z - g + 1) & (DEPTH - 1))


def add_to(acc, slot, value):
    spot = acc.at[pl.ds(pl.multiple_of(slot * HALF, HALF), HALF), :]
    spot[...] = spot[...] + value


def add_strip(left, strip, accs, slot_of, count):
    both = jnp.dot(left, strip, preferred_element_type=F32)
    low = lax.broadcasted_iota(jnp.int32, (HALF, LANES), 1) < W
    for e in range(0, count, 2):
        even = both[:HALF, W * e : W * e + LANES]
        odd = both[HALF:, W * e : W * e + LANES]
        add_to(accs[0], slot_of(e), jnp.where(low, even, pltpu.roll(odd, W, 1)))
        if e + 1 < count:
            add_to(accs[1], slot_of(e + 1), jnp.where(low, pltpu.roll(even, W, 1), odd))


def near_kernel(
    blocks, own, cols, slots, far, acc_a, acc_b, table, left,
    held, prolong, cols_v, slots_v, look, double, strip, sems, row_sems,
):
    small = [
        pltpu.make_async_copy(source, target, sems.at[n])
        for n, (source, target) in enumerate(((cols, cols_v), (slots, slots_v), (own, prolong)))
    ]
    for copy in small:
        copy.start()

    def fetches(z):
        return [
            pltpu.make_async_copy(blocks.at[i], held.at[i], row_sems.at[i]) for i in (z, z + DEPTH)
        ]

    def request(step):
        for z in STEPS[step][0]:
            for copy in fetches(z):
                copy.start()

    for step in range(AHEAD):
        request(step)
    acc_a[...] = jnp.zeros_like(acc_a)
    acc_b[...] = jnp.zeros_like(acc_b)
    small[0].wait()
    small[1].wait()
    table[...] = ordered(cols_v[...], slots_v[...])
    to_look = pltpu.make_async_copy(table, look, sems.at[3])
    to_look.start()
    small[2].wait()
    r = lax.broadcasted_iota(jnp.int32, (W, W), 0)
    c = lax.broadcasted_iota(jnp.int32, (W, W), 1)
    split = (c == (r % HALF) * 2 + r // HALF).astype(F32).astype(BF)
    for i in range(ROWS):
        p = prolong[i]
        double[i] = jnp.concatenate([p, p], axis=1)
        left[i] = lax.dot_general(
            split, p, (((1,), (1,)), ((), ())), preferred_element_type=F32
        ).astype(BF)
    to_look.wait()

    def block(i, d, u, g):
        return held[i, look[i, d * 9 + u * 3 + g] >> 6]

    def repack(z):
        for x in range(2):
            for u in range(3):
                for g in range(3):
                    at = (u * 3 + g) * W
                    side = LANES * (x if u == 0 else 1 - x)
                    i = x * DEPTH + z
                    pair = jnp.concatenate([block(i, 0, u, g), block(i, 2, u, g)], axis=1)
                    far[(z + g - 1) & (DEPTH - 1), at : at + W, side : side + LANES] = pair

    def local(z):
        for x in range(2):
            users = [(user(x, u, g, z), u, g) for u in range(3) for g in range(3)]
            stack = jnp.concatenate([block(i, 1, u, g) for i, u, g in users], axis=0)
            applied = jnp.dot(stack, double[x * DEPTH + z], preferred_element_type=F32).astype(BF)
            for e, (i, u, g) in enumerate(users):
                lane = W * (e % 2)
                strip[i, :, W * e : W * e + W] = applied[W * e : W * e + W, lane : lane + W]

    def finish(z):
        for i in (z, z + DEPTH):
            add_strip(left[i], strip[i], (acc_a, acc_b), lambda e: look[i, 9 + e] & (W - 1), 9)

    for step, (arrived, complete, ready) in enumerate(STEPS):
        for z in arrived:
            for copy in fetches(z):
                copy.wait()
        if step + AHEAD < len(STEPS):
            request(step + AHEAD)
        for z in ready:
            finish(z)
        for z in arrived:
            repack(z)
        for z in complete:
            local(z)


def far_kernel(
    table, blocks, near_a, near_b, left, after, before, up, mid, down,
    acc_a, acc_b, look, lows, highs, strip, sems,
):
    to_look = pltpu.make_async_copy(table, look, sems.at[0])
    to_look.start()
    none = jnp.zeros((W, W), BF)
    blank = jnp.zeros((W, LANES), BF)
    for j in range(ROWS):
        lows[j] = jnp.concatenate([before[j], none], axis=1)
        highs[j] = jnp.concatenate([none, after[j]], axis=1)
    part = acc_a.shape[0] // DEPTH

    def multiply(z, carry):
        rows = pl.ds(pl.multiple_of(z * part, part), part)
        acc_a[rows, :] = near_a[rows, :]
        acc_b[rows, :] = near_b[rows, :]
        four = [
            jnp.concatenate([lows[z], blank], axis=1),
            jnp.concatenate([highs[z], blank], axis=1),
            jnp.concatenate([blank, lows[DEPTH + z]], axis=1),
            jnp.concatenate([blank, highs[DEPTH + z]], axis=1),
        ]
        diagonal = jnp.concatenate(four, axis=0)
        applied = jnp.dot(blocks[z], diagonal, preferred_element_type=F32).astype(BF)
        for u in range(3):
            for g in range(3):
                at = (u * 3 + g) * W
                for x in range(2):
                    part_of = applied[at : at + W, LANES * x : LANES * x + LANES]
                    strip[user(x, u, g, z), :, 2 * at : 2 * at + LANES] = part_of
        return carry

    lax.fori_loop(0, DEPTH, multiply, 0, unroll=UNROLL_FAR)
    to_look.wait()

    def finish(i, carry):
        add_strip(
            left[i], strip[i], (acc_a, acc_b), lambda e: look[i, e // 2 + 18 * (e % 2)] & (W - 1), 18
        )
        return carry

    lax.fori_loop(0, ROWS, finish, 0, unroll=UNROLL_STRIP)
    for n, out in enumerate((down, mid, up)):
        rows = slice(n * BUF * HALF, (n + 1) * BUF * HALF)
        out[...] = (acc_a[rows, :] + acc_b[rows, :]).astype(out.dtype)


def by_tile(source, blocks):
    groups = [
        jnp.concatenate([source[HALF * m + 8 * n : HALF * m + 8 * n + 8, :] for m in range(blocks)], axis=0)
        for n in range(HALF // 8)
    ]
    return jnp.concatenate(groups, axis=1)


def route_kernel(into, mid, pick, kept):
    chosen = jnp.broadcast_to(into[...], (8, 3 * BUF)).astype(F32).astype(BF)

    def one_hot(blocks, source):
        lanes = 8 * blocks
        block = lax.broadcasted_iota(jnp.int32, (3 * BUF, lanes), 1) // 8
        entry = lax.broadcasted_iota(jnp.int32, (3 * BUF, lanes), 0)
        spread = (entry == source(block)).astype(F32).astype(BF)
        owner = jnp.dot(chosen, spread, preferred_element_type=F32)[0:1]
        place = lax.broadcasted_iota(jnp.int32, (SLOTS, lanes), 0).astype(F32)
        hit = jnp.where(jnp.broadcast_to(owner, (SLOTS, lanes)) == place, 1.0, 0.0)
        row = lax.broadcasted_iota(jnp.int32, (SLOTS, lanes), 1) & 7
        return jnp.concatenate([jnp.where(row == t, hit, 0.0) for t in range(8)], axis=0).astype(BF)

    pick[...] = one_hot(2 * BUF, lambda block: jnp.where(block < BUF, block, block + BUF))
    own = one_hot(BUF, lambda block: block + BUF)
    value = by_tile(mid, BUF)
    top = value.astype(BF)
    rest = value - top.astype(F32)
    middle = rest.astype(BF)
    last = (rest - middle.astype(F32)).astype(BF)
    sums = [jnp.dot(own, part, preferred_element_type=F32) for part in (top, middle, last)]
    kept[...] = sums[0] + sums[1] + sums[2]


def gather_kernel(pick, kept, right, left, out):
    arrived = jnp.concatenate([by_tile(left, BUF), by_tile(right, BUF)], axis=0)
    sums = kept[...] + jnp.dot(pick[...], arrived, preferred_element_type=F32)
    for n in range(HALF // 8):
        for t in range(8):
            at = LANES * (8 * n + t)
            out[:, at : at + LANES] = sums[SLOTS * t : SLOTS * t + SLOTS, LANES * n : LANES * n + LANES]


HBM = pl.BlockSpec(memory_space=pltpu.HBM)
VMEM = pl.BlockSpec(memory_space=pltpu.VMEM)
SMEM = pl.BlockSpec(memory_space=pltpu.SMEM)
SUMS = jax.ShapeDtypeStruct((3 * BUF * HALF, LANES), F32)
THIRD = (BUF * HALF, LANES)
TABLE = (ROWS, NBR)
WIDE = pltpu.VMEM((ROWS, W, LANES), BF)


def near(*operands):
    return pl.pallas_call(
        near_kernel,
        out_shape=(
            jax.ShapeDtypeStruct((DEPTH, 9 * W, 4 * W), BF),
            SUMS,
            SUMS,
            jax.ShapeDtypeStruct(TABLE, jnp.int32),
            jax.ShapeDtypeStruct((ROWS, W, W), BF),
        ),
        in_specs=[HBM] * 4,
        out_specs=(VMEM,) * 5,
        scratch_shapes=[
            pltpu.VMEM((ROWS, NBR, W, W), BF),
            pltpu.VMEM((ROWS, W, W), BF),
            pltpu.VMEM(TABLE, jnp.int32),
            pltpu.VMEM(TABLE, jnp.int32),
            pltpu.SMEM(TABLE, jnp.int32),
            WIDE,
            pltpu.VMEM((ROWS, W, 10 * W), BF),
            pltpu.SemaphoreType.DMA((4,)),
            pltpu.SemaphoreType.DMA((ROWS,)),
        ],
        compiler_params=pltpu.CompilerParams(vmem_limit_bytes=40 << 20),
        cost_estimate=pl.CostEstimate(flops=10**9, bytes_accessed=12 * 10**6, transcendentals=0),
        name="near",
    )(*(pltpu.with_memory_space_constraint(value, pltpu.HBM) for value in operands))


def far(*operands):
    sent = jax.ShapeDtypeStruct(THIRD, BF)
    return pl.pallas_call(
        far_kernel,
        out_shape=(sent, jax.ShapeDtypeStruct(THIRD, F32), sent),
        in_specs=[VMEM] * 7,
        out_specs=(VMEM,) * 3,
        scratch_shapes=[
            pltpu.VMEM(SUMS.shape, F32),
            pltpu.VMEM(SUMS.shape, F32),
            pltpu.SMEM(TABLE, jnp.int32),
            WIDE,
            WIDE,
            pltpu.VMEM((ROWS, W, 18 * W), BF),
            pltpu.SemaphoreType.DMA((1,)),
        ],
        compiler_params=pltpu.CompilerParams(vmem_limit_bytes=24 << 20),
        name="far",
    )(*operands)


def route(*operands):
    rows = 8 * SLOTS
    return pl.pallas_call(
        route_kernel,
        out_shape=(
            jax.ShapeDtypeStruct((rows, 16 * BUF), BF),
            jax.ShapeDtypeStruct((rows, LANES * HALF // 8), F32),
        ),
        in_specs=[VMEM, VMEM],
        out_specs=(VMEM, VMEM),
        compiler_params=pltpu.CompilerParams(vmem_limit_bytes=24 << 20),
        cost_estimate=pl.CostEstimate(flops=10**9, bytes_accessed=10**7, transcendentals=0),
        name="route",
    )(*operands)


def gather(*operands):
    return pl.pallas_call(
        gather_kernel,
        out_shape=jax.ShapeDtypeStruct((SLOTS, W * W), F32),
        in_specs=[VMEM] * 4,
        out_specs=VMEM,
        compiler_params=pltpu.CompilerParams(vmem_limit_bytes=16 << 20),
        name="gather",
    )(*operands)


def per_device(matrix_blocks, prolong, columns, partial_slot, into_slot):
    before = shifted(prolong, "inner", 1)
    after = shifted(prolong, "inner", -1)
    blocks, acc_a, acc_b, table, left = near(matrix_blocks, prolong, columns, partial_slot)
    up, mid, down = far(table, blocks, acc_a, acc_b, left, after, before)
    from_left = shifted(up, "slab", 1)
    from_right = shifted(down, "slab", -1)
    pick, kept = route(into_slot, mid)
    return gather(pick, kept, from_right, from_left)


def solution(mesh):
    return jax.shard_map(
        per_device,
        mesh=mesh,
        in_specs=(
            P(("slab", "inner"), None, None, None),
            P(("slab", "inner"), None, None),
            P(("slab", "inner"), None),
            P(("slab", "inner"), None),
            P(("slab", "inner"), None),
        ),
        out_specs=P(("slab", "inner"), None),
        check_vma=False,
    )
```

```python
import jax
import jax.numpy as jnp
from jax import lax
from jax.experimental import pallas as pl
from jax.experimental.pallas import tpu as pltpu
from jax.sharding import PartitionSpec as P

W = 64
HALF = W // 2
LANES = 2 * W
NBR = 27
ROWS = 16
DEPTH = 8
BUF = 16
SLOTS = 32
LAYERS = 64
F32 = jnp.float32
BF = jnp.bfloat16
UNROLL_FAR, UNROLL_STRIP = 8, 16
AHEAD = 4
STEPS = (
    ((7, 0), (), ()),
    ((1,), (0,), ()),
    ((2,), (1,), ()),
    ((3,), (2,), ()),
    ((4,), (3,), (1,)),
    ((5,), (4,), (2,)),
    ((6,), (5, 6, 7), (3,)),
    ((), (), (0, 4, 5, 6, 7)),
)


def shifted(value, axis, steps):
    count = lax.axis_size(axis)
    pairs = [(source, (source + steps) % count) for source in range(count)]
    return lax.ppermute(value, axis, pairs)


def ordered(cols, slots):
    row = lax.broadcasted_iota(jnp.int32, cols.shape, 0)
    k = lax.broadcasted_iota(jnp.int32, cols.shape, 1)
    layer = (cols >> 4) & (LAYERS - 1)
    own = jnp.broadcast_to(layer[:, 0:1], cols.shape)
    d = (layer - own + 1) & (LAYERS - 1)
    other = ((cols >> 3) & 1) ^ (row >> 3)
    g = ((cols & 7) - (row & 7) + 1) & 7
    key = d * 6 + other * 3 + g
    value = (k * W + slots).astype(F32)
    table = jnp.zeros(cols.shape, F32)
    for d in range(3):
        for g in range(3):
            one = jnp.min(jnp.where(key == d * 6 + g, value, 1e9), axis=1, keepdims=True)
            two = key == d * 6 + 3 + g
            low = jnp.min(jnp.where(two, value, 1e9), axis=1, keepdims=True)
            high = jnp.max(jnp.where(two, value, -1.0), axis=1, keepdims=True)
            for u, found in enumerate((one, low, high)):
                table = jnp.where(k == d * 9 + u * 3 + g, found, table)
    return table.astype(jnp.int32)


def user(x, u, g, z):
    return (x if u == 0 else 1 - x) * DEPTH + ((z - g + 1) & (DEPTH - 1))


def add_to(acc, slot, value):
    spot = acc.at[pl.ds(pl.multiple_of(slot * HALF, HALF), HALF), :]
    spot[...] = spot[...] + value


def add_strip(left, strip, accs, slot_of, count):
    both = jnp.dot(left, strip, preferred_element_type=F32)
    low = lax.broadcasted_iota(jnp.int32, (HALF, LANES), 1) < W
    for e in range(0, count, 2):
        even = both[:HALF, W * e : W * e + LANES]
        odd = both[HALF:, W * e : W * e + LANES]
        add_to(accs[0], slot_of(e), jnp.where(low, even, pltpu.roll(odd, W, 1)))
        if e + 1 < count:
            add_to(accs[1], slot_of(e + 1), jnp.where(low, pltpu.roll(even, W, 1), odd))


def near_kernel(
    blocks, own, cols, slots, far, acc_a, acc_b, table, left,
    held, prolong, cols_v, slots_v, look, double, strip, sems, row_sems,
):
    small = [
        pltpu.make_async_copy(source, target, sems.at[n])
        for n, (source, target) in enumerate(((cols, cols_v), (slots, slots_v), (own, prolong)))
    ]
    for copy in small:
        copy.start()

    def fetches(z):
        return [
            pltpu.make_async_copy(blocks.at[i], held.at[i], row_sems.at[i]) for i in (z, z + DEPTH)
        ]

    def request(step):
        for z in STEPS[step][0]:
            for copy in fetches(z):
                copy.start()

    for step in range(AHEAD):
        request(step)
    acc_a[...] = jnp.zeros_like(acc_a)
    acc_b[...] = jnp.zeros_like(acc_b)
    small[0].wait()
    small[1].wait()
    table[...] = ordered(cols_v[...], slots_v[...])
    to_look = pltpu.make_async_copy(table, look, sems.at[3])
    to_look.start()
    small[2].wait()
    r = lax.broadcasted_iota(jnp.int32, (W, W), 0)
    c = lax.broadcasted_iota(jnp.int32, (W, W), 1)
    split = (c == (r % HALF) * 2 + r // HALF).astype(F32).astype(BF)
    for i in range(ROWS):
        p = prolong[i]
        double[i] = jnp.concatenate([p, p], axis=1)
        left[i] = lax.dot_general(
            split, p, (((1,), (1,)), ((), ())), preferred_element_type=F32
        ).astype(BF)
    to_look.wait()

    def block(i, d, u, g):
        return held[i, look[i, d * 9 + u * 3 + g] >> 6]

    def repack(z):
        for x in range(2):
            for u in range(3):
                for g in range(3):
                    at = (u * 3 + g) * W
                    side = LANES * (x if u == 0 else 1 - x)
                    i = x * DEPTH + z
                    pair = jnp.concatenate([block(i, 0, u, g), block(i, 2, u, g)], axis=1)
                    far[(z + g - 1) & (DEPTH - 1), at : at + W, side : side + LANES] = pair

    def local(z):
        for x in range(2):
            users = [(user(x, u, g, z), u, g) for u in range(3) for g in range(3)]
            stack = jnp.concatenate([block(i, 1, u, g) for i, u, g in users], axis=0)
            applied = jnp.dot(stack, double[x * DEPTH + z], preferred_element_type=F32).astype(BF)
            for e, (i, u, g) in enumerate(users):
                lane = W * (e % 2)
                strip[i, :, W * e : W * e + W] = applied[W * e : W * e + W, lane : lane + W]

    def finish(z):
        for i in (z, z + DEPTH):
            add_strip(left[i], strip[i], (acc_a, acc_b), lambda e: look[i, 9 + e] & (W - 1), 9)

    for step, (arrived, complete, ready) in enumerate(STEPS):
        for z in arrived:
            for copy in fetches(z):
                copy.wait()
        if step + AHEAD < len(STEPS):
            request(step + AHEAD)
        for z in ready:
            finish(z)
        for z in arrived:
            repack(z)
        for z in complete:
            local(z)


def far_kernel(
    table, blocks, near_a, near_b, left, after, before, up, mid, down,
    acc_a, acc_b, look, lows, highs, strip, sems,
):
    to_look = pltpu.make_async_copy(table, look, sems.at[0])
    to_look.start()
    none = jnp.zeros((W, W), BF)
    blank = jnp.zeros((W, LANES), BF)
    for j in range(ROWS):
        lows[j] = jnp.concatenate([before[j], none], axis=1)
        highs[j] = jnp.concatenate([none, after[j]], axis=1)
    part = acc_a.shape[0] // DEPTH

    def multiply(z, carry):
        rows = pl.ds(pl.multiple_of(z * part, part), part)
        acc_a[rows, :] = near_a[rows, :]
        acc_b[rows, :] = near_b[rows, :]
        four = [
            jnp.concatenate([lows[z], blank], axis=1),
            jnp.concatenate([highs[z], blank], axis=1),
            jnp.concatenate([blank, lows[DEPTH + z]], axis=1),
            jnp.concatenate([blank, highs[DEPTH + z]], axis=1),
        ]
        diagonal = jnp.concatenate(four, axis=0)
        applied = jnp.dot(blocks[z], diagonal, preferred_element_type=F32).astype(BF)
        for u in range(3):
            for g in range(3):
                at = (u * 3 + g) * W
                for x in range(2):
                    part_of = applied[at : at + W, LANES * x : LANES * x + LANES]
                    strip[user(x, u, g, z), :, 2 * at : 2 * at + LANES] = part_of
        return carry

    lax.fori_loop(0, DEPTH, multiply, 0, unroll=UNROLL_FAR)
    to_look.wait()

    def finish(i, carry):
        add_strip(
            left[i], strip[i], (acc_a, acc_b), lambda e: look[i, e // 2 + 18 * (e % 2)] & (W - 1), 18
        )
        return carry

    lax.fori_loop(0, ROWS, finish, 0, unroll=UNROLL_STRIP)
    for n, out in enumerate((down, mid, up)):
        rows = slice(n * BUF * HALF, (n + 1) * BUF * HALF)
        out[...] = (acc_a[rows, :] + acc_b[rows, :]).astype(out.dtype)


def by_tile(source, blocks):
    groups = [
        jnp.concatenate([source[HALF * m + 8 * n : HALF * m + 8 * n + 8, :] for m in range(blocks)], axis=0)
        for n in range(HALF // 8)
    ]
    return jnp.concatenate(groups, axis=1)


def route_kernel(into, mid, pick, kept):
    chosen = jnp.broadcast_to(into[...], (8, 3 * BUF)).astype(F32).astype(BF)

    def one_hot(blocks, source):
        lanes = 8 * blocks
        block = lax.broadcasted_iota(jnp.int32, (3 * BUF, lanes), 1) // 8
        entry = lax.broadcasted_iota(jnp.int32, (3 * BUF, lanes), 0)
        spread = (entry == source(block)).astype(F32).astype(BF)
        owner = jnp.dot(chosen, spread, preferred_element_type=F32)[0:1]
        place = lax.broadcasted_iota(jnp.int32, (SLOTS, lanes), 0).astype(F32)
        hit = jnp.where(jnp.broadcast_to(owner, (SLOTS, lanes)) == place, 1.0, 0.0)
        row = lax.broadcasted_iota(jnp.int32, (SLOTS, lanes), 1) & 7
        return jnp.concatenate([jnp.where(row == t, hit, 0.0) for t in range(8)], axis=0).astype(BF)

    pick[...] = one_hot(2 * BUF, lambda block: jnp.where(block < BUF, block, block + BUF))
    own = one_hot(BUF, lambda block: block + BUF)
    value = by_tile(mid, BUF)
    top = value.astype(BF)
    rest = value - top.astype(F32)
    middle = rest.astype(BF)
    last = (rest - middle.astype(F32)).astype(BF)
    sums = [jnp.dot(own, part, preferred_element_type=F32) for part in (top, middle, last)]
    kept[...] = sums[0] + sums[1] + sums[2]


def gather_kernel(pick, kept, left, right, out):
    arrived = jnp.concatenate([by_tile(left, BUF), by_tile(right, BUF)], axis=0)
    sums = kept[...] + jnp.dot(pick[...], arrived, preferred_element_type=F32)
    for n in range(HALF // 8):
        for t in range(8):
            at = LANES * (8 * n + t)
            out[:, at : at + LANES] = sums[SLOTS * t : SLOTS * t + SLOTS, LANES * n : LANES * n + LANES]


HBM = pl.BlockSpec(memory_space=pltpu.HBM)
VMEM = pl.BlockSpec(memory_space=pltpu.VMEM)
SMEM = pl.BlockSpec(memory_space=pltpu.SMEM)
SUMS = jax.ShapeDtypeStruct((3 * BUF * HALF, LANES), F32)
THIRD = (BUF * HALF, LANES)
TABLE = (ROWS, NBR)
WIDE = pltpu.VMEM((ROWS, W, LANES), BF)


def near(*operands):
    return pl.pallas_call(
        near_kernel,
        out_shape=(
            jax.ShapeDtypeStruct((DEPTH, 9 * W, 4 * W), BF),
            SUMS,
            SUMS,
            jax.ShapeDtypeStruct(TABLE, jnp.int32),
            jax.ShapeDtypeStruct((ROWS, W, W), BF),
        ),
        in_specs=[HBM] * 4,
        out_specs=(VMEM,) * 5,
        scratch_shapes=[
            pltpu.VMEM((ROWS, NBR, W, W), BF),
            pltpu.VMEM((ROWS, W, W), BF),
            pltpu.VMEM(TABLE, jnp.int32),
            pltpu.VMEM(TABLE, jnp.int32),
            pltpu.SMEM(TABLE, jnp.int32),
            WIDE,
            pltpu.VMEM((ROWS, W, 10 * W), BF),
            pltpu.SemaphoreType.DMA((4,)),
            pltpu.SemaphoreType.DMA((ROWS,)),
        ],
        compiler_params=pltpu.CompilerParams(vmem_limit_bytes=40 << 20),
        cost_estimate=pl.CostEstimate(flops=10**9, bytes_accessed=12 * 10**6, transcendentals=0),
        name="near",
    )(*(pltpu.with_memory_space_constraint(value, pltpu.HBM) for value in operands))


def far(*operands):
    sent = jax.ShapeDtypeStruct(THIRD, BF)
    return pl.pallas_call(
        far_kernel,
        out_shape=(sent, jax.ShapeDtypeStruct(THIRD, F32), sent),
        in_specs=[VMEM] * 7,
        out_specs=(VMEM,) * 3,
        scratch_shapes=[
            pltpu.VMEM(SUMS.shape, F32),
            pltpu.VMEM(SUMS.shape, F32),
            pltpu.SMEM(TABLE, jnp.int32),
            WIDE,
            WIDE,
            pltpu.VMEM((ROWS, W, 18 * W), BF),
            pltpu.SemaphoreType.DMA((1,)),
        ],
        compiler_params=pltpu.CompilerParams(vmem_limit_bytes=24 << 20),
        name="far",
    )(*operands)


def route(*operands):
    rows = 8 * SLOTS
    return pl.pallas_call(
        route_kernel,
        out_shape=(
            jax.ShapeDtypeStruct((rows, 16 * BUF), BF),
            jax.ShapeDtypeStruct((rows, LANES * HALF // 8), F32),
        ),
        in_specs=[VMEM, VMEM],
        out_specs=(VMEM, VMEM),
        compiler_params=pltpu.CompilerParams(vmem_limit_bytes=24 << 20),
        cost_estimate=pl.CostEstimate(flops=10**9, bytes_accessed=10**7, transcendentals=0),
        name="route",
    )(*operands)


def gather(*operands):
    return pl.pallas_call(
        gather_kernel,
        out_shape=jax.ShapeDtypeStruct((SLOTS, W * W), F32),
        in_specs=[VMEM] * 4,
        out_specs=VMEM,
        compiler_params=pltpu.CompilerParams(vmem_limit_bytes=16 << 20),
        name="gather",
    )(*operands)


def per_device(matrix_blocks, prolong, columns, partial_slot, into_slot):
    before = shifted(prolong, "inner", 1)
    after = shifted(prolong, "inner", -1)
    blocks, acc_a, acc_b, table, left = near(matrix_blocks, prolong, columns, partial_slot)
    up, mid, down = far(table, blocks, acc_a, acc_b, left, after, before)
    from_left = shifted(up, "slab", 1)
    from_right = shifted(down, "slab", -1)
    pick, kept = route(into_slot, mid)
    return gather(pick, kept, from_left, from_right)


def solution(mesh):
    return jax.shard_map(
        per_device,
        mesh=mesh,
        in_specs=(
            P(("slab", "inner"), None, None, None),
            P(("slab", "inner"), None, None),
            P(("slab", "inner"), None),
            P(("slab", "inner"), None),
            P(("slab", "inner"), None),
        ),
        out_specs=P(("slab", "inner"), None),
        check_vma=False,
    )
```

```python
import jax
import jax.numpy as jnp
from jax import lax
from jax.experimental import pallas as pl
from jax.experimental.pallas import tpu as pltpu
from jax.sharding import PartitionSpec as P

W = 64
HALF = W // 2
LANES = 2 * W
NBR = 27
ROWS = 16
DEPTH = 8
BUF = 16
SLOTS = 32
LAYERS = 64
F32 = jnp.float32
BF = jnp.bfloat16
UNROLL_FAR, UNROLL_STRIP = 8, 16
FIRST, SECOND = 2, 5
STEPS = (
    ((7, 0), (), ()),
    ((1,), (0,), ()),
    ((2,), (1,), ()),
    ((3,), (2,), ()),
    ((4,), (3,), (1,)),
    ((5,), (4,), (2,)),
    ((6,), (5, 6, 7), (3,)),
    ((), (), (0, 4, 5, 6, 7)),
)


def shifted(value, axis, steps):
    count = lax.axis_size(axis)
    pairs = [(source, (source + steps) % count) for source in range(count)]
    return lax.ppermute(value, axis, pairs)


def ordered(cols, slots):
    row = lax.broadcasted_iota(jnp.int32, cols.shape, 0)
    k = lax.broadcasted_iota(jnp.int32, cols.shape, 1)
    layer = (cols >> 4) & (LAYERS - 1)
    own = jnp.broadcast_to(layer[:, 0:1], cols.shape)
    d = (layer - own + 1) & (LAYERS - 1)
    other = ((cols >> 3) & 1) ^ (row >> 3)
    g = ((cols & 7) - (row & 7) + 1) & 7
    key = d * 6 + other * 3 + g
    value = (k * W + slots).astype(F32)
    table = jnp.zeros(cols.shape, F32)
    for d in range(3):
        for g in range(3):
            one = jnp.min(jnp.where(key == d * 6 + g, value, 1e9), axis=1, keepdims=True)
            two = key == d * 6 + 3 + g
            low = jnp.min(jnp.where(two, value, 1e9), axis=1, keepdims=True)
            high = jnp.max(jnp.where(two, value, -1.0), axis=1, keepdims=True)
            for u, found in enumerate((one, low, high)):
                table = jnp.where(k == d * 9 + u * 3 + g, found, table)
    return table.astype(jnp.int32)


def user(x, u, g, z):
    return (x if u == 0 else 1 - x) * DEPTH + ((z - g + 1) & (DEPTH - 1))


def add_to(acc, slot, value):
    spot = acc.at[pl.ds(pl.multiple_of(slot * HALF, HALF), HALF), :]
    spot[...] = spot[...] + value


def add_strip(left, strip, accs, slot_of, count):
    both = jnp.dot(left, strip, preferred_element_type=F32)
    low = lax.broadcasted_iota(jnp.int32, (HALF, LANES), 1) < W
    for e in range(0, count, 2):
        even = both[:HALF, W * e : W * e + LANES]
        turned = pltpu.roll(both[HALF:, W * e : W * e + LANES], W, 1)
        add_to(accs[0], slot_of(e), jnp.where(low, even, turned))
        if e + 1 < count:
            add_to(accs[1], slot_of(e + 1), jnp.where(low, turned, even))


def near_kernel(
    blocks, own, cols, slots, far, acc_a, acc_b, table, left,
    held, prolong, cols_v, slots_v, look, double, strip, sems, row_sems,
):
    small = [
        pltpu.make_async_copy(source, target, sems.at[n])
        for n, (source, target) in enumerate(((cols, cols_v), (slots, slots_v), (own, prolong)))
    ]
    for copy in small:
        copy.start()

    def fetches(z):
        return [
            pltpu.make_async_copy(blocks.at[i], held.at[i], row_sems.at[i]) for i in (z, z + DEPTH)
        ]

    def request(step):
        for z in STEPS[step][0]:
            for copy in fetches(z):
                copy.start()

    for step in range(FIRST):
        request(step)
    acc_a[...] = jnp.zeros_like(acc_a)
    acc_b[...] = jnp.zeros_like(acc_b)
    small[0].wait()
    small[1].wait()
    for step in range(FIRST, SECOND):
        request(step)
    table[...] = ordered(cols_v[...], slots_v[...])
    to_look = pltpu.make_async_copy(table, look, sems.at[3])
    to_look.start()
    small[2].wait()
    r = lax.broadcasted_iota(jnp.int32, (W, W), 0)
    c = lax.broadcasted_iota(jnp.int32, (W, W), 1)
    split = (c == (r % HALF) * 2 + r // HALF).astype(F32).astype(BF)
    for i in range(ROWS):
        p = prolong[i]
        double[i] = jnp.concatenate([p, p], axis=1)
        left[i] = lax.dot_general(
            split, p, (((1,), (1,)), ((), ())), preferred_element_type=F32
        ).astype(BF)
    for step in range(SECOND, len(STEPS)):
        request(step)
    to_look.wait()

    def block(i, d, u, g):
        return held[i, look[i, d * 9 + u * 3 + g] >> 6]

    def repack(z):
        for x in range(2):
            for u in range(3):
                for g in range(3):
                    at = (u * 3 + g) * W
                    side = LANES * (x if u == 0 else 1 - x)
                    i = x * DEPTH + z
                    pair = jnp.concatenate([block(i, 0, u, g), block(i, 2, u, g)], axis=1)
                    far[(z + g - 1) & (DEPTH - 1), at : at + W, side : side + LANES] = pair

    def local(z):
        for x in range(2):
            users = [(user(x, u, g, z), u, g) for u in range(3) for g in range(3)]
            stack = jnp.concatenate([block(i, 1, u, g) for i, u, g in users], axis=0)
            applied = jnp.dot(stack, double[x * DEPTH + z], preferred_element_type=F32).astype(BF)
            for e, (i, u, g) in enumerate(users):
                lane = W * (e % 2)
                strip[i, :, W * e : W * e + W] = applied[W * e : W * e + W, lane : lane + W]

    def finish(z):
        for i in (z, z + DEPTH):
            add_strip(left[i], strip[i], (acc_a, acc_b), lambda e: look[i, 9 + e] & (W - 1), 9)

    for step, (arrived, complete, ready) in enumerate(STEPS):
        for z in arrived:
            for copy in fetches(z):
                copy.wait()
        for z in ready:
            finish(z)
        for z in arrived:
            repack(z)
        for z in complete:
            local(z)


def far_kernel(
    table, blocks, near_a, near_b, left, after, before, up, mid, down,
    acc_a, acc_b, look, lows, highs, strip, sems,
):
    to_look = pltpu.make_async_copy(table, look, sems.at[0])
    to_look.start()
    none = jnp.zeros((W, W), BF)
    blank = jnp.zeros((W, LANES), BF)
    for j in range(ROWS):
        lows[j] = jnp.concatenate([before[j], none], axis=1)
        highs[j] = jnp.concatenate([none, after[j]], axis=1)
    part = acc_a.shape[0] // DEPTH

    def multiply(z, carry):
        rows = pl.ds(pl.multiple_of(z * part, part), part)
        acc_a[rows, :] = near_a[rows, :]
        acc_b[rows, :] = near_b[rows, :]
        four = [
            jnp.concatenate([lows[z], blank], axis=1),
            jnp.concatenate([highs[z], blank], axis=1),
            jnp.concatenate([blank, lows[DEPTH + z]], axis=1),
            jnp.concatenate([blank, highs[DEPTH + z]], axis=1),
        ]
        diagonal = jnp.concatenate(four, axis=0)
        applied = jnp.dot(blocks[z], diagonal, preferred_element_type=F32).astype(BF)
        for u in range(3):
            for g in range(3):
                at = (u * 3 + g) * W
                for x in range(2):
                    part_of = applied[at : at + W, LANES * x : LANES * x + LANES]
                    strip[user(x, u, g, z), :, 2 * at : 2 * at + LANES] = part_of
        return carry

    lax.fori_loop(0, DEPTH, multiply, 0, unroll=UNROLL_FAR)
    to_look.wait()

    def finish(i, carry):
        add_strip(
            left[i], strip[i], (acc_a, acc_b), lambda e: look[i, e // 2 + 18 * (e % 2)] & (W - 1), 18
        )
        return carry

    lax.fori_loop(0, ROWS, finish, 0, unroll=UNROLL_STRIP)
    for n, out in enumerate((down, mid, up)):
        rows = slice(n * BUF * HALF, (n + 1) * BUF * HALF)
        out[...] = (acc_a[rows, :] + pltpu.roll(acc_b[rows, :], W, 1)).astype(out.dtype)


def by_tile(source, blocks):
    groups = [
        jnp.concatenate([source[HALF * m + 8 * n : HALF * m + 8 * n + 8, :] for m in range(blocks)], axis=0)
        for n in range(HALF // 8)
    ]
    return jnp.concatenate(groups, axis=1)


def route_kernel(into, mid, pick, kept):
    chosen = jnp.broadcast_to(into[...], (8, 3 * BUF)).astype(F32).astype(BF)

    def one_hot(blocks, source):
        lanes = 8 * blocks
        block = lax.broadcasted_iota(jnp.int32, (3 * BUF, lanes), 1) // 8
        entry = lax.broadcasted_iota(jnp.int32, (3 * BUF, lanes), 0)
        spread = (entry == source(block)).astype(F32).astype(BF)
        owner = jnp.dot(chosen, spread, preferred_element_type=F32)[0:1]
        place = lax.broadcasted_iota(jnp.int32, (SLOTS, lanes), 0).astype(F32)
        hit = jnp.where(jnp.broadcast_to(owner, (SLOTS, lanes)) == place, 1.0, 0.0)
        row = lax.broadcasted_iota(jnp.int32, (SLOTS, lanes), 1) & 7
        return jnp.concatenate([jnp.where(row == t, hit, 0.0) for t in range(8)], axis=0).astype(BF)

    pick[...] = one_hot(2 * BUF, lambda block: jnp.where(block < BUF, block, block + BUF))
    own = one_hot(BUF, lambda block: block + BUF)
    value = by_tile(mid, BUF)
    top = value.astype(BF)
    rest = value - top.astype(F32)
    middle = rest.astype(BF)
    last = (rest - middle.astype(F32)).astype(BF)
    sums = [jnp.dot(own, part, preferred_element_type=F32) for part in (top, middle, last)]
    kept[...] = sums[0] + sums[1] + sums[2]


def gather_kernel(pick, kept, left, right, out):
    arrived = jnp.concatenate([by_tile(left, BUF), by_tile(right, BUF)], axis=0)
    sums = kept[...] + jnp.dot(pick[...], arrived, preferred_element_type=F32)
    for n in range(HALF // 8):
        for t in range(8):
            at = LANES * (8 * n + t)
            out[:, at : at + LANES] = sums[SLOTS * t : SLOTS * t + SLOTS, LANES * n : LANES * n + LANES]


HBM = pl.BlockSpec(memory_space=pltpu.HBM)
VMEM = pl.BlockSpec(memory_space=pltpu.VMEM)
SMEM = pl.BlockSpec(memory_space=pltpu.SMEM)
SUMS = jax.ShapeDtypeStruct((3 * BUF * HALF, LANES), F32)
THIRD = (BUF * HALF, LANES)
TABLE = (ROWS, NBR)
WIDE = pltpu.VMEM((ROWS, W, LANES), BF)


def near(*operands):
    return pl.pallas_call(
        near_kernel,
        out_shape=(
            jax.ShapeDtypeStruct((DEPTH, 9 * W, 4 * W), BF),
            SUMS,
            SUMS,
            jax.ShapeDtypeStruct(TABLE, jnp.int32),
            jax.ShapeDtypeStruct((ROWS, W, W), BF),
        ),
        in_specs=[HBM] * 4,
        out_specs=(VMEM,) * 5,
        scratch_shapes=[
            pltpu.VMEM((ROWS, NBR, W, W), BF),
            pltpu.VMEM((ROWS, W, W), BF),
            pltpu.VMEM(TABLE, jnp.int32),
            pltpu.VMEM(TABLE, jnp.int32),
            pltpu.SMEM(TABLE, jnp.int32),
            WIDE,
            pltpu.VMEM((ROWS, W, 10 * W), BF),
            pltpu.SemaphoreType.DMA((4,)),
            pltpu.SemaphoreType.DMA((ROWS,)),
        ],
        compiler_params=pltpu.CompilerParams(vmem_limit_bytes=40 << 20),
        cost_estimate=pl.CostEstimate(flops=10**9, bytes_accessed=12 * 10**6, transcendentals=0),
        name="near",
    )(*(pltpu.with_memory_space_constraint(value, pltpu.HBM) for value in operands))


def far(*operands):
    sent = jax.ShapeDtypeStruct(THIRD, BF)
    return pl.pallas_call(
        far_kernel,
        out_shape=(sent, jax.ShapeDtypeStruct(THIRD, F32), sent),
        in_specs=[VMEM] * 7,
        out_specs=(VMEM,) * 3,
        scratch_shapes=[
            pltpu.VMEM(SUMS.shape, F32),
            pltpu.VMEM(SUMS.shape, F32),
            pltpu.SMEM(TABLE, jnp.int32),
            WIDE,
            WIDE,
            pltpu.VMEM((ROWS, W, 18 * W), BF),
            pltpu.SemaphoreType.DMA((1,)),
        ],
        compiler_params=pltpu.CompilerParams(vmem_limit_bytes=24 << 20),
        name="far",
    )(*operands)


def route(*operands):
    rows = 8 * SLOTS
    return pl.pallas_call(
        route_kernel,
        out_shape=(
            jax.ShapeDtypeStruct((rows, 16 * BUF), BF),
            jax.ShapeDtypeStruct((rows, LANES * HALF // 8), F32),
        ),
        in_specs=[VMEM, VMEM],
        out_specs=(VMEM, VMEM),
        compiler_params=pltpu.CompilerParams(vmem_limit_bytes=24 << 20),
        cost_estimate=pl.CostEstimate(flops=10**9, bytes_accessed=10**7, transcendentals=0),
        name="route",
    )(*operands)


def gather(*operands):
    return pl.pallas_call(
        gather_kernel,
        out_shape=jax.ShapeDtypeStruct((SLOTS, W * W), F32),
        in_specs=[VMEM] * 4,
        out_specs=VMEM,
        compiler_params=pltpu.CompilerParams(vmem_limit_bytes=16 << 20),
        name="gather",
    )(*operands)


def per_device(matrix_blocks, prolong, columns, partial_slot, into_slot):
    before = shifted(prolong, "inner", 1)
    after = shifted(prolong, "inner", -1)
    blocks, acc_a, acc_b, table, left = near(matrix_blocks, prolong, columns, partial_slot)
    up, mid, down = far(table, blocks, acc_a, acc_b, left, after, before)
    from_left = shifted(up, "slab", 1)
    from_right = shifted(down, "slab", -1)
    pick, kept = route(into_slot, mid)
    return gather(pick, kept, from_left, from_right)


def solution(mesh):
    return jax.shard_map(
        per_device,
        mesh=mesh,
        in_specs=(
            P(("slab", "inner"), None, None, None),
            P(("slab", "inner"), None, None),
            P(("slab", "inner"), None),
            P(("slab", "inner"), None),
            P(("slab", "inner"), None),
        ),
        out_specs=P(("slab", "inner"), None),
        check_vma=False,
    )
```

```python
import jax
import jax.numpy as jnp
from jax import lax
from jax.experimental import pallas as pl
from jax.experimental.pallas import tpu as pltpu
from jax.sharding import PartitionSpec as P

W = 64
HALF = W // 2
LANES = 2 * W
NBR = 27
ROWS = 16
DEPTH = 8
BUF = 16
SLOTS = 32
LAYERS = 64
F32 = jnp.float32
BF = jnp.bfloat16
UNROLL_FAR, UNROLL_STRIP = 8, 16
FIRST, SECOND = 2, 5
STEPS = (
    ((7, 0), (), ()),
    ((1,), (0,), ()),
    ((2,), (1,), ()),
    ((3,), (2,), ()),
    ((4,), (3,), (1,)),
    ((5,), (4,), (2,)),
    ((6,), (5, 6, 7), (3,)),
    ((), (), (0, 4, 5, 6, 7)),
)


def shifted(value, axis, steps):
    count = lax.axis_size(axis)
    pairs = [(source, (source + steps) % count) for source in range(count)]
    return lax.ppermute(value, axis, pairs)


def ordered(cols, slots):
    row = lax.broadcasted_iota(jnp.int32, cols.shape, 0)
    k = lax.broadcasted_iota(jnp.int32, cols.shape, 1)
    layer = (cols >> 4) & (LAYERS - 1)
    own = jnp.broadcast_to(layer[:, 0:1], cols.shape)
    d = (layer - own + 1) & (LAYERS - 1)
    other = ((cols >> 3) & 1) ^ (row >> 3)
    g = ((cols & 7) - (row & 7) + 1) & 7
    key = d * 6 + other * 3 + g
    value = (k * W + slots).astype(F32)
    table = jnp.zeros(cols.shape, F32)
    for d in range(3):
        for g in range(3):
            one = jnp.min(jnp.where(key == d * 6 + g, value, 1e9), axis=1, keepdims=True)
            two = key == d * 6 + 3 + g
            low = jnp.min(jnp.where(two, value, 1e9), axis=1, keepdims=True)
            high = jnp.max(jnp.where(two, value, -1.0), axis=1, keepdims=True)
            for u, found in enumerate((one, low, high)):
                table = jnp.where(k == d * 9 + u * 3 + g, found, table)
    return table.astype(jnp.int32)


def user(x, u, g, z):
    return (x if u == 0 else 1 - x) * DEPTH + ((z - g + 1) & (DEPTH - 1))


def add_to(acc, slot, value):
    spot = acc.at[pl.ds(pl.multiple_of(slot * HALF, HALF), HALF), :]
    spot[...] = spot[...] + value


def add_strip(left, strip, accs, slot_of, count):
    both = jnp.dot(left, strip, preferred_element_type=F32)
    low = lax.broadcasted_iota(jnp.int32, (HALF, LANES), 1) < W
    for e in range(0, count, 2):
        even = both[:HALF, W * e : W * e + LANES]
        turned = pltpu.roll(both[HALF:, W * e : W * e + LANES], W, 1)
        add_to(accs[0], slot_of(e), jnp.where(low, even, turned))
        if e + 1 < count:
            add_to(accs[1], slot_of(e + 1), jnp.where(low, turned, even))


def near_kernel(
    blocks, own, cols, slots, far, acc_a, acc_b, table, left,
    held, prolong, cols_v, slots_v, look, double, strip, sems, row_sems,
):
    small = [
        pltpu.make_async_copy(source, target, sems.at[n])
        for n, (source, target) in enumerate(((cols, cols_v), (slots, slots_v), (own, prolong)))
    ]
    for copy in small:
        copy.start()

    def fetches(z):
        return [
            pltpu.make_async_copy(blocks.at[i], held.at[i], row_sems.at[i]) for i in (z, z + DEPTH)
        ]

    def request(step):
        for z in STEPS[step][0]:
            for copy in fetches(z):
                copy.start()

    for step in range(FIRST):
        request(step)
    acc_a[...] = jnp.zeros_like(acc_a)
    acc_b[...] = jnp.zeros_like(acc_b)
    small[0].wait()
    small[1].wait()
    for step in range(FIRST, SECOND):
        request(step)
    table[...] = ordered(cols_v[...], slots_v[...])
    to_look = pltpu.make_async_copy(table, look, sems.at[3])
    to_look.start()
    small[2].wait()
    r = lax.broadcasted_iota(jnp.int32, (W, W), 0)
    c = lax.broadcasted_iota(jnp.int32, (W, W), 1)
    split = (c == (r % HALF) * 2 + r // HALF).astype(F32).astype(BF)
    for i in range(ROWS):
        p = prolong[i]
        double[i] = jnp.concatenate([p, p], axis=1)
        left[i] = lax.dot_general(
            split, p, (((1,), (1,)), ((), ())), preferred_element_type=F32
        ).astype(BF)
    for step in range(SECOND, len(STEPS)):
        request(step)
    to_look.wait()

    def block(i, d, u, g):
        return held[i, look[i, d * 9 + u * 3 + g] >> 6]

    def repack(z):
        for x in range(2):
            for u in range(3):
                for g in range(3):
                    at = (u * 3 + g) * W
                    side = LANES * (x if u == 0 else 1 - x)
                    i = x * DEPTH + z
                    pair = jnp.concatenate([block(i, 0, u, g), block(i, 2, u, g)], axis=1)
                    far[(z + g - 1) & (DEPTH - 1), at : at + W, side : side + LANES] = pair

    def local(z):
        for x in range(2):
            users = [(user(x, u, g, z), u, g) for u in range(3) for g in range(3)]
            stack = jnp.concatenate([block(i, 1, u, g) for i, u, g in users], axis=0)
            applied = jnp.dot(stack, double[x * DEPTH + z], preferred_element_type=F32).astype(BF)
            for e, (i, u, g) in enumerate(users):
                lane = W * (e % 2)
                strip[i, :, W * e : W * e + W] = applied[W * e : W * e + W, lane : lane + W]

    def finish(z):
        for i in (z, z + DEPTH):
            add_strip(left[i], strip[i], (acc_a, acc_b), lambda e: look[i, 9 + e] & (W - 1), 9)

    for step, (arrived, complete, ready) in enumerate(STEPS):
        for z in arrived:
            for copy in fetches(z):
                copy.wait()
        for z in ready:
            finish(z)
        for z in arrived:
            repack(z)
        for z in complete:
            local(z)


def far_kernel(
    table, blocks, near_a, near_b, left, after, before, up, mid_a, mid_b, down,
    acc_a, acc_b, look, lows, highs, strip, sems,
):
    to_look = pltpu.make_async_copy(table, look, sems.at[0])
    to_look.start()
    none = jnp.zeros((W, W), BF)
    blank = jnp.zeros((W, LANES), BF)
    for j in range(ROWS):
        lows[j] = jnp.concatenate([before[j], none], axis=1)
        highs[j] = jnp.concatenate([none, after[j]], axis=1)
    part = acc_a.shape[0] // DEPTH

    def multiply(z, carry):
        rows = pl.ds(pl.multiple_of(z * part, part), part)
        acc_a[rows, :] = near_a[rows, :]
        acc_b[rows, :] = near_b[rows, :]
        four = [
            jnp.concatenate([lows[z], blank], axis=1),
            jnp.concatenate([highs[z], blank], axis=1),
            jnp.concatenate([blank, lows[DEPTH + z]], axis=1),
            jnp.concatenate([blank, highs[DEPTH + z]], axis=1),
        ]
        diagonal = jnp.concatenate(four, axis=0)
        applied = jnp.dot(blocks[z], diagonal, preferred_element_type=F32).astype(BF)
        for u in range(3):
            for g in range(3):
                at = (u * 3 + g) * W
                for x in range(2):
                    part_of = applied[at : at + W, LANES * x : LANES * x + LANES]
                    strip[user(x, u, g, z), :, 2 * at : 2 * at + LANES] = part_of
        return carry

    lax.fori_loop(0, DEPTH, multiply, 0, unroll=UNROLL_FAR)
    to_look.wait()

    def finish(i, carry):
        add_strip(
            left[i], strip[i], (acc_a, acc_b), lambda e: look[i, e // 2 + 18 * (e % 2)] & (W - 1), 18
        )
        return carry

    lax.fori_loop(0, ROWS, finish, 0, unroll=UNROLL_STRIP)
    for n, out in ((2, up), (0, down)):
        rows = slice(n * BUF * HALF, (n + 1) * BUF * HALF)
        out[...] = (acc_a[rows, :] + pltpu.roll(acc_b[rows, :], W, 1)).astype(out.dtype)
    rows = slice(BUF * HALF, 2 * BUF * HALF)
    mid_a[...] = acc_a[rows, :]
    mid_b[...] = acc_b[rows, :]


def by_tile(source, blocks):
    groups = [
        jnp.concatenate([source[HALF * m + 8 * n : HALF * m + 8 * n + 8, :] for m in range(blocks)], axis=0)
        for n in range(HALF // 8)
    ]
    return jnp.concatenate(groups, axis=1)


def route_kernel(into, mid_a, mid_b, pick, kept):
    chosen = jnp.broadcast_to(into[...], (8, 3 * BUF)).astype(F32).astype(BF)

    def one_hot(blocks, source):
        lanes = 8 * blocks
        block = lax.broadcasted_iota(jnp.int32, (3 * BUF, lanes), 1) // 8
        entry = lax.broadcasted_iota(jnp.int32, (3 * BUF, lanes), 0)
        spread = (entry == source(block)).astype(F32).astype(BF)
        owner = jnp.dot(chosen, spread, preferred_element_type=F32)[0:1]
        place = lax.broadcasted_iota(jnp.int32, (SLOTS, lanes), 0).astype(F32)
        hit = jnp.where(jnp.broadcast_to(owner, (SLOTS, lanes)) == place, 1.0, 0.0)
        row = lax.broadcasted_iota(jnp.int32, (SLOTS, lanes), 1) & 7
        return jnp.concatenate([jnp.where(row == t, hit, 0.0) for t in range(8)], axis=0).astype(BF)

    pick[...] = one_hot(2 * BUF, lambda block: jnp.where(block < BUF, block, block + BUF))
    own = one_hot(BUF, lambda block: block + BUF)
    value = by_tile(mid_a[...] + pltpu.roll(mid_b[...], W, 1), BUF)
    top = value.astype(BF)
    rest = value - top.astype(F32)
    middle = rest.astype(BF)
    last = (rest - middle.astype(F32)).astype(BF)
    sums = [jnp.dot(own, part, preferred_element_type=F32) for part in (top, middle, last)]
    kept[...] = sums[0] + sums[1] + sums[2]


def gather_kernel(pick, kept, left, right, out):
    arrived = jnp.concatenate([by_tile(left, BUF), by_tile(right, BUF)], axis=0)
    sums = kept[...] + jnp.dot(pick[...], arrived, preferred_element_type=F32)
    for n in range(HALF // 8):
        for t in range(8):
            at = LANES * (8 * n + t)
            out[:, at : at + LANES] = sums[SLOTS * t : SLOTS * t + SLOTS, LANES * n : LANES * n + LANES]


HBM = pl.BlockSpec(memory_space=pltpu.HBM)
VMEM = pl.BlockSpec(memory_space=pltpu.VMEM)
SMEM = pl.BlockSpec(memory_space=pltpu.SMEM)
SUMS = jax.ShapeDtypeStruct((3 * BUF * HALF, LANES), F32)
THIRD = (BUF * HALF, LANES)
TABLE = (ROWS, NBR)
WIDE = pltpu.VMEM((ROWS, W, LANES), BF)


def near(*operands):
    return pl.pallas_call(
        near_kernel,
        out_shape=(
            jax.ShapeDtypeStruct((DEPTH, 9 * W, 4 * W), BF),
            SUMS,
            SUMS,
            jax.ShapeDtypeStruct(TABLE, jnp.int32),
            jax.ShapeDtypeStruct((ROWS, W, W), BF),
        ),
        in_specs=[HBM] * 4,
        out_specs=(VMEM,) * 5,
        scratch_shapes=[
            pltpu.VMEM((ROWS, NBR, W, W), BF),
            pltpu.VMEM((ROWS, W, W), BF),
            pltpu.VMEM(TABLE, jnp.int32),
            pltpu.VMEM(TABLE, jnp.int32),
            pltpu.SMEM(TABLE, jnp.int32),
            WIDE,
            pltpu.VMEM((ROWS, W, 10 * W), BF),
            pltpu.SemaphoreType.DMA((4,)),
            pltpu.SemaphoreType.DMA((ROWS,)),
        ],
        compiler_params=pltpu.CompilerParams(vmem_limit_bytes=40 << 20),
        cost_estimate=pl.CostEstimate(flops=10**9, bytes_accessed=12 * 10**6, transcendentals=0),
        name="near",
    )(*(pltpu.with_memory_space_constraint(value, pltpu.HBM) for value in operands))


def far(*operands):
    sent = jax.ShapeDtypeStruct(THIRD, BF)
    own = jax.ShapeDtypeStruct(THIRD, F32)
    return pl.pallas_call(
        far_kernel,
        out_shape=(sent, own, own, sent),
        in_specs=[VMEM] * 7,
        out_specs=(VMEM,) * 4,
        scratch_shapes=[
            pltpu.VMEM(SUMS.shape, F32),
            pltpu.VMEM(SUMS.shape, F32),
            pltpu.SMEM(TABLE, jnp.int32),
            WIDE,
            WIDE,
            pltpu.VMEM((ROWS, W, 18 * W), BF),
            pltpu.SemaphoreType.DMA((1,)),
        ],
        compiler_params=pltpu.CompilerParams(vmem_limit_bytes=24 << 20),
        name="far",
    )(*operands)


def route(*operands):
    rows = 8 * SLOTS
    return pl.pallas_call(
        route_kernel,
        out_shape=(
            jax.ShapeDtypeStruct((rows, 16 * BUF), BF),
            jax.ShapeDtypeStruct((rows, LANES * HALF // 8), F32),
        ),
        in_specs=[VMEM] * 3,
        out_specs=(VMEM, VMEM),
        compiler_params=pltpu.CompilerParams(vmem_limit_bytes=24 << 20),
        cost_estimate=pl.CostEstimate(flops=10**9, bytes_accessed=10**7, transcendentals=0),
        name="route",
    )(*operands)


def gather(*operands):
    return pl.pallas_call(
        gather_kernel,
        out_shape=jax.ShapeDtypeStruct((SLOTS, W * W), F32),
        in_specs=[VMEM] * 4,
        out_specs=VMEM,
        compiler_params=pltpu.CompilerParams(vmem_limit_bytes=16 << 20),
        name="gather",
    )(*operands)


def per_device(matrix_blocks, prolong, columns, partial_slot, into_slot):
    before = shifted(prolong, "inner", 1)
    after = shifted(prolong, "inner", -1)
    blocks, acc_a, acc_b, table, left = near(matrix_blocks, prolong, columns, partial_slot)
    up, mid_a, mid_b, down = far(table, blocks, acc_a, acc_b, left, after, before)
    from_left = shifted(up, "slab", 1)
    from_right = shifted(down, "slab", -1)
    pick, kept = route(into_slot, mid_a, mid_b)
    return gather(pick, kept, from_left, from_right)


def solution(mesh):
    return jax.shard_map(
        per_device,
        mesh=mesh,
        in_specs=(
            P(("slab", "inner"), None, None, None),
            P(("slab", "inner"), None, None),
            P(("slab", "inner"), None),
            P(("slab", "inner"), None),
            P(("slab", "inner"), None),
        ),
        out_specs=P(("slab", "inner"), None),
        check_vma=False,
    )
```
